256 devices in a mesh: dp: 32 (over x, z_hi, y), col: 8 (over z_lo, core).
Axes of the slice: x: 4, y: 4, z: 8 (z_hi: 2, z_lo: 4; z = z_hi * 4 + z_lo), core: 2. Of those that a mesh axis runs over, the one named last changes fastest.
Arguments:
- embeddings: bfloat16 [16384, 4096], P('dp'), may hold values from -16 to 16
- rotation: bfloat16 [4096, 4096], P(None, 'col'), may hold values from -0.09375 to 0.09375
- codes: int32 [16384, 512], P('dp', 'col'), may hold values from 0 to 255
- codebooks: bfloat16 [512, 256, 8], P('col'), may hold values from -16 to 16
Outputs:
- new_rotation: float32 [4096, 4096], P('dp', 'col')
The draws below stay inside these ranges and needn't reach their ends.
All inputs are finite; a program needn't handle non-finite values.
Results may differ from the reference program's by a relative error of at most 0.015.
Values may be sent and summed in bfloat16 or wider, within the bound.
A program may use at most 64 MiB of HBM per device.

```python
import math
import jax
import jax.numpy as jnp
from jax import lax

D = 4096
DS = 8
K = 256
STEPS = 2
M = 512
ROWS = 16384
N_DP = 32


def draw_embeddings(key, part):
    key_scale, key_vals = jax.random.split(key, 2)
    ramp = jnp.arange(D, dtype=jnp.float32) / D
    spread = jax.random.uniform(key_scale, (D,), jnp.float32)
    col_scale = 0.3 * jnp.exp(math.log(10.0) * (0.5 * ramp + 0.5 * spread))
    values = jnp.clip(jax.random.normal(key_vals, (ROWS, D), jnp.float32), -4.0, 4.0)
    return (values * col_scale[None, :]).astype(jnp.bfloat16)


def draw_codebooks(key, part):
    key_scale, key_vals = jax.random.split(key, 2)
    ramp = jnp.arange(M, dtype=jnp.float32) / M
    spread = jax.random.uniform(key_scale, (M,), jnp.float32)
    sub_scale = 0.3 * jnp.exp(math.log(10.0) * (0.5 * ramp + 0.5 * spread))
    values = jnp.clip(jax.random.normal(key_vals, (M, K, DS), jnp.float32), -4.0, 4.0)
    return (values * sub_scale[:, None, None]).astype(jnp.bfloat16)


def touch_ends(result, stream_key, smallest, largest):
    longest = result.shape.index(max(result.shape))
    spots = []
    for shift in (0, 1):
        where = [jax.random.randint(jax.random.fold_in(stream_key, axis), (), 0, length) for axis, length in enumerate(result.shape)]
        where[longest] = (where[longest] + shift) % result.shape[longest]
        spots.append(tuple(where))
    return result.at[spots[0]].set(smallest).at[spots[1]].set(largest)


def block_scale(rng, shape, cuts, low, largest):
    factor_of, own = 1.0, jax.random.fold_in(rng, 6)
    for axis_at, blocks in cuts:
        steps = jnp.exp(jax.random.uniform(jax.random.fold_in(own, axis_at), (blocks,), jnp.float32, low / len(cuts), largest / len(cuts)))
        factor_of = factor_of * jnp.repeat(steps, shape[axis_at] // blocks).reshape([-1 if axis == axis_at else 1 for axis in range(len(shape))])
    return factor_of


def centred(rng, shape, scale, limit, cuts=(), held_as=jnp.bfloat16):
    loudness = block_scale(rng, shape, cuts, -0.22, 0.18) if cuts else 1.0
    array = jax.random.normal(rng, shape, jnp.float32) * scale * loudness
    return jnp.minimum(jnp.maximum(array, -limit), limit).astype(held_as)


def setup_inputs(seed: int = 0) -> dict:
    key_list = jax.random.split(jax.random.key(seed), 5)
    embeddings = draw_embeddings(jax.random.fold_in(key_list[4], 71), 0)
    rotation = centred(key_list[1], (D, D), D ** -0.5, 0.09375, ((1, 8),))
    codes = touch_ends(jax.random.randint(key_list[2], (ROWS, M), 0, K), jax.random.fold_in(key_list[2], 1), 0, K - 1).astype(jnp.int32)
    codebooks = draw_codebooks(jax.random.fold_in(key_list[4], 71), 0)
    return {"embeddings": embeddings, "rotation": rotation, "codes": codes, "codebooks": codebooks}


def reference(embeddings, rotation, codes, codebooks):
    rotated = jnp.dot(embeddings, rotation, preferred_element_type=jnp.float32)
    sub_index = jnp.arange(M, dtype=jnp.int32)[None, :]
    picked = codebooks[sub_index, codes]
    rebuilt = picked.reshape(ROWS, D)
    residue = rotated - rebuilt.astype(jnp.float32)
    row_error = lax.optimization_barrier(jnp.sum(residue * residue, axis=1))
    weights = 1.0 / (1.0 + row_error / (2.0 * D))
    weighted = (weights[:, None] * rebuilt.astype(jnp.float32)).astype(jnp.bfloat16)
    cross = jnp.dot(embeddings.T, weighted, preferred_element_type=jnp.float32)
    cross = cross + 0.2 * ROWS * rotation.astype(jnp.float32)
    norm_scale = 1.4 * jnp.sqrt(jnp.sum(cross * cross) / D)
    iterate = cross / norm_scale
    for step_index in range(STEPS):
        half_iter = iterate.astype(jnp.bfloat16)
        blocks = half_iter.reshape(N_DP, D // N_DP, D)

        def add_block(running, row_block):
            gram_term = jnp.dot(row_block.T, row_block, preferred_element_type=jnp.float32)
            rounded = lax.optimization_barrier(gram_term.astype(jnp.bfloat16))
            return (running + rounded.astype(jnp.float32), None)
        gram, unused = lax.scan(add_block, jnp.zeros((D, D), jnp.float32), blocks)
        product = jnp.dot(half_iter, gram.astype(jnp.bfloat16), preferred_element_type=jnp.float32)
        iterate = 1.5 * iterate - 0.5 * product
    return D ** 0.5 * iterate
```

```python
import functools
import math

import jax
import jax.numpy as jnp
from jax import lax
from jax.experimental import pallas as pl
from jax.experimental.pallas import tpu as pltpu
from jax.sharding import PartitionSpec as P

MESH = pl.DeviceIdType.MESH
BF = jnp.bfloat16
F32 = jnp.float32
NX, NY, NZH, NZL, NC = 4, 4, 2, 4, 2
NSEM = 256


def rebuild_rows(codes, codebooks):
    tok_rows, sub_count = codes.shape
    centroids = codebooks.shape[1]
    sub_width = codebooks.shape[2]
    group_size = min(16, sub_count)
    centroid_ids = jnp.arange(centroids, dtype=jnp.int32)
    diag_eye = jnp.eye(group_size, dtype=jnp.bfloat16)
    pieces = []
    for first_sub in range(0, sub_count, group_size):
        sub_ids = codes[:, first_sub : first_sub + group_size]
        onehot = (sub_ids[:, :, None] == centroid_ids[None, None, :]).astype(jnp.bfloat16)
        onehot = onehot.reshape(tok_rows, group_size * centroids)
        block_table = (
            codebooks[first_sub : first_sub + group_size][:, :, None, :]
            * diag_eye[:, None, :, None]
        )
        block_table = block_table.reshape(group_size * centroids, group_size * sub_width)
        pieces.append(
            jnp.dot(onehot, block_table, preferred_element_type=jnp.float32).astype(jnp.bfloat16)
        )
    return jnp.concatenate(pieces, axis=1)


def dot_nt(a, b):
    return lax.dot_general(a, b, (((1,), (1,)), ((), ())), preferred_element_type=F32)


def dot_nn(a, b):
    return jnp.dot(a, b, preferred_element_type=F32)


class Place:
    def __init__(self):
        dp, col = lax.axis_index("dp"), lax.axis_index("col")
        self.x = dp // (NZH * NY)
        self.zh = (dp // NY) % NZH
        self.y = dp % NY
        self.zl = col // NC
        self.c = col % NC
        self.z = self.zh * NZL + self.zl

    def at(self, dx=0, dy=0, dz=0, dc=0):
        x = (self.x + dx) % NX
        y = (self.y + dy) % NY
        z = (self.z + dz) % (NZH * NZL)
        c = (self.c + dc) % NC
        return (x * (NZH * NY) + (z // NZL) * NY + y, (z % NZL) * NC + c)

    def along(self, axis, step):
        return self.at(dx=step) if axis == "x" else self.at(dy=step)

    def index(self, axis):
        return self.x if axis == "x" else self.y


class Sems:
    def __init__(self, send, recv):
        self.send, self.recv, self.used = send, recv, 0

    def take(self, count=1):
        base = self.used
        self.used += count
        assert self.used <= NSEM
        return base

    def copy(self, src, dst, index, device):
        return pltpu.make_async_remote_copy(
            src_ref=src,
            dst_ref=dst,
            send_sem=self.send.at[index],
            recv_sem=self.recv.at[index],
            device_id=device,
            device_id_type=MESH,
        )


def ring_scatter(place, sems, axis, chunk, out, keep, diag, got, to_r, to_l, from_l, from_r):
    rows = diag.shape[0]
    half = rows // 2
    lo, hi = pl.ds(0, half), pl.ds(half, half)
    p = place.index(axis)
    right, left = place.along(axis, 1), place.along(axis, -1)
    s = sems.take(6)
    chunk((p + 2) % 4)
    diag[...] = keep[...].astype(BF)
    c0 = sems.copy(diag.at[lo], got.at[lo], s, right)
    c1 = sems.copy(diag.at[hi], got.at[hi], s + 1, left)
    c0.start()
    c1.start()
    yield
    chunk((p + 1) % 4)
    to_r[hi] = keep[hi].astype(BF)
    c2 = sems.copy(to_r.at[hi], from_l.at[hi], s + 2, right)
    c2.start()
    c0.wait_recv()
    to_r[lo] = (keep[lo] + got[lo].astype(F32)).astype(BF)
    c3 = sems.copy(to_r.at[lo], from_l.at[lo], s + 3, right)
    c3.start()
    yield
    chunk((p + 3) % 4)
    to_l[lo] = keep[lo].astype(BF)
    c4 = sems.copy(to_l.at[lo], from_r.at[lo], s + 4, left)
    c4.start()
    c1.wait_recv()
    to_l[hi] = (keep[hi] + got[hi].astype(F32)).astype(BF)
    c5 = sems.copy(to_l.at[hi], from_r.at[hi], s + 5, left)
    c5.start()
    yield
    chunk(p)
    for c in (c2, c3, c4, c5):
        c.wait_recv()
    out[...] = keep[...] + from_l[...].astype(F32) + from_r[...].astype(F32)
    for c in (c0, c1, c2, c3, c4, c5):
        c.wait_send()
    yield


def ring_gather(place, sems, axis, buf):
    half = buf.shape[1] // 2
    lo, hi = pl.ds(0, half), pl.ds(half, half)
    p = place.index(axis)
    right, left = place.along(axis, 1), place.along(axis, -1)
    s = sems.take(4)
    before, after = (p + 3) % 4, (p + 1) % 4
    c0 = sems.copy(buf.at[p], buf.at[p], s, right)
    c1 = sems.copy(buf.at[p], buf.at[p], s + 1, left)
    c0.start()
    c1.start()
    yield
    c0.wait_recv()
    c2 = sems.copy(buf.at[before, lo], buf.at[before, lo], s + 2, right)
    c2.start()
    c1.wait_recv()
    c3 = sems.copy(buf.at[after, hi], buf.at[after, hi], s + 3, left)
    c3.start()
    yield
    c2.wait_recv()
    c3.wait_recv()
    for c in (c0, c1, c2, c3):
        c.wait_send()
    yield


def run(*gens):
    live = list(gens)
    while live:
        for g in list(live):
            try:
                next(g)
            except StopIteration:
                live.remove(g)


def spread_z(place, sems, bt, at):
    z, c = place.z, place.c
    d = (place.zl - place.y + 4) % 4
    back = (4 - d) % 4
    up, down, other = place.at(dz=1), place.at(dz=-1), place.at(dc=1)
    up_origin = ((z - d + 8) % 8) // 4
    down_origin = ((z + back) % 8) // 4
    half = at.shape[3] // 2
    lo, hi = pl.ds(0, half), pl.ds(half, half)
    far = 1 - place.zh
    s_up, s_down = sems.take(4), sems.take(4)
    s_up_half, s_down_half = sems.take(4), sems.take(4)
    s_core = sems.take(8)

    def core_copy(origin, q):
        return sems.copy(at.at[origin, c, q], at.at[origin, c, q], s_core + origin * 4 + q, other)

    @pl.when(d == 0)
    def _():
        at[place.zh, c] = bt[...]

    def up_full(q):
        return sems.copy(at.at[up_origin, c, q], at.at[up_origin, c, q], s_up + q, up)

    def down_full(q):
        return sems.copy(at.at[down_origin, c, q], at.at[down_origin, c, q], s_down + q, down)

    def up_half(q):
        return sems.copy(at.at[up_origin, c, q, lo], at.at[up_origin, c, q, lo], s_up_half + q, up)

    def down_half(q):
        return sems.copy(at.at[down_origin, c, q, hi], at.at[down_origin, c, q, hi], s_down_half + q, down)

    for t in range(8):
        q_up = t - d

        @pl.when((q_up >= 0) & (q_up < 4))
        def _(q_up=q_up):
            @pl.when(d > 0)
            def _():
                up_full(q_up).wait_recv()

            @pl.when(d < 3)
            def _():
                up_full(q_up).start()

            @pl.when(d == 3)
            def _():
                up_half(q_up).start()

            core_copy(up_origin, q_up).start()

        q_down = t - back

        @pl.when((q_down >= 0) & (q_down < 4))
        def _(q_down=q_down):
            @pl.when(d > 0)
            def _():
                down_full(q_down).wait_recv()

            @pl.when(d != 1)
            def _():
                down_full(q_down).start()

            @pl.when(d == 1)
            def _():
                down_half(q_down).start()

            @pl.when(d > 0)
            def _():
                core_copy(down_origin, q_down).start()

        if t >= 4:

            @pl.when(d == 0)
            def _(q=t - 4):
                sems.copy(at.at[far, c, q, lo], at.at[far, c, q, lo], s_up_half + q, up).wait_recv()
                sems.copy(at.at[far, c, q, hi], at.at[far, c, q, hi], s_down_half + q, down).wait_recv()
                core_copy(far, q).start()

    for origin in range(2):
        for q in range(4):
            pltpu.make_async_remote_copy(
                src_ref=at.at[origin, 1 - c, q],
                dst_ref=at.at[origin, 1 - c, q],
                send_sem=sems.send.at[s_core + origin * 4 + q],
                recv_sem=sems.recv.at[s_core + origin * 4 + q],
                device_id=other,
                device_id_type=MESH,
            ).wait()
    for q in range(4):

        @pl.when(d < 3)
        def _(q=q):
            up_full(q).wait_send()

        @pl.when(d == 3)
        def _(q=q):
            up_half(q).wait_send()

        @pl.when(d != 1)
        def _(q=q):
            down_full(q).wait_send()

        @pl.when(d == 1)
        def _(q=q):
            down_half(q).wait_send()


def share_sum(place, sems, mine, slots, partners):
    s = sems.take(len(partners))
    copies = [sems.copy(mine, slots.at[i], s + i, device) for i, device in enumerate(partners)]
    for c in copies:
        c.start()
    return copies


def finish_sum(copies, mine, slots):
    for c in copies:
        c.wait()
    total = mine[...]
    for i in range(len(copies)):
        total = total + slots[i]
    return total


def main_kernel(
    prior_scale, width, wt, e, prior, out,
    keep_a, keep_b, big, small, own_a, own_b, ab, ab_out, ab_in, xo, red,
    bt, at, gkeep, gbuf, gown, gfull, ykeep, ybuf, sq, sq_in, last_out, last_in,
    send, recv,
):
    place = Place()
    sems = Sems(send, recv)
    barrier = pltpu.get_barrier_semaphore()
    partners = (
        [place.at(dx=i) for i in (1, 2, 3)]
        + [place.at(dy=i) for i in (1, 2, 3)]
        + [place.at(dz=i) for i in range(1, 8)]
        + [place.at(dc=1)]
    )
    for device in partners:
        pl.semaphore_signal(barrier, inc=1, device_id=device, device_id_type=MESH)
    pl.semaphore_wait(barrier, len(partners))

    block = out.shape[2]
    n_half = wt.shape[0] // 2
    x_cols = e.shape[1] // NX

    def chunk_a(xi):
        start = pl.multiple_of(xi * x_cols, x_cols)
        value = dot_nn(wt[0:n_half], e[:, pl.ds(start, x_cols)])
        for zh in range(NZH):
            for y in range(NY):
                at_in, at_out = (zh * NY + y) * block, (y * NZH + zh) * block
                keep_a[:, at_out : at_out + block] = value[:, at_in : at_in + block]

    def chunk_b(yi):
        parts = []
        for x in range(NX):
            for zh in range(NZH):
                start = pl.multiple_of(x * x_cols + (zh * NY + yi) * block, block)
                parts.append(e[:, pl.ds(start, block)])
        keep_b[...] = dot_nn(wt[n_half:], jnp.concatenate(parts, axis=1))

    def piece(source, keep):
        def chunk(i):
            width_of = keep.shape[1]
            keep[...] = source[:, pl.ds(pl.multiple_of(i * width_of, width_of), width_of)]

        return chunk

    run(
        ring_scatter(place, sems, "x", chunk_a, own_a, keep_a, *[big.at[0, i] for i in range(6)]),
        ring_scatter(place, sems, "y", chunk_b, own_b, keep_b, *[big.at[1, i] for i in range(6)]),
    )
    run(
        ring_scatter(place, sems, "y", piece(own_a, red.at[0]), ab.at[0], red.at[0], *[small.at[0, i] for i in range(6)]),
        ring_scatter(place, sems, "x", piece(own_b, red.at[1]), ab.at[1], red.at[1], *[small.at[1, i] for i in range(6)]),
    )
    ab_out[...] = ab[1 - place.zh].astype(BF)
    s = sems.take()
    swap = sems.copy(ab_out, ab_in, s, place.at(dz=4))
    swap.start()
    swap.wait()
    x_new = ab[place.zh] + ab_in[...].astype(F32) + prior_scale * prior[...]
    xo[...] = x_new
    squares = x_new * x_new
    folded = jnp.sum(squares.reshape(squares.shape[0] // 8, 8, squares.shape[1]), axis=0)
    part = folded[:, 0:128]
    for i in range(1, folded.shape[1] // 128):
        part = part + folded[:, i * 128 : (i + 1) * 128]
    sq[0] = part

    y_copies = share_sum(place, sems, sq.at[0], sq_in.at[0], [place.at(dy=i) for i in (1, 2, 3)])
    inv = None
    for step in range(2):
        b_ref, a_ref, g_ref = bt.at[step], at.at[step], gfull.at[step]
        b_ref[place.y] = xo[...].astype(BF)
        run(ring_gather(place, sems, "y", b_ref))
        if step == 0:
            sq[1] = finish_sum(y_copies, sq.at[0], sq_in.at[0])
            z_copies = share_sum(place, sems, sq.at[1], sq_in.at[1], [place.at(dz=i) for i in range(1, 8)])
        spread_z(place, sems, b_ref, a_ref)
        if step == 0:
            sq[2] = finish_sum(z_copies, sq.at[1], sq_in.at[1])
            c_copies = share_sum(place, sems, sq.at[2], sq_in.at[2], [place.at(dc=1)])
        for i in range(NZH * NC):
            total = None
            for q in range(NY):
                term = dot_nt(b_ref[q], a_ref[i // NC, i % NC, q])
                total = term if total is None else total + term
            w = total.shape[1]
            gkeep[0, :, i * w : (i + 1) * w] = total
        g_rows = gkeep.shape[1] // NX

        def chunk_g(xi):
            gkeep[1, 0:g_rows] = gkeep[0, pl.ds(pl.multiple_of(xi * g_rows, g_rows), g_rows)]

        run(
            ring_scatter(
                place, sems, "x", chunk_g, gown, gkeep.at[1, 0:g_rows], *[gbuf.at[step, i] for i in range(6)]
            )
        )
        if step == 0:
            sq[3] = finish_sum(c_copies, sq.at[2], sq_in.at[2])
            x_copies = share_sum(place, sems, sq.at[3], sq_in.at[3], [place.at(dx=i) for i in (1, 2, 3)])
        g_ref[place.x] = gown[...].astype(BF)
        run(ring_gather(place, sems, "x", g_ref))
        if step == 0:
            total = jnp.sum(finish_sum(x_copies, sq.at[3], sq_in.at[3]))
            scale2 = jnp.full((8, 128), 1.96 / width, F32) * total
            inv = 1.0 / jnp.sqrt(scale2)
        gram = jnp.concatenate([g_ref[i] for i in range(NX)], axis=0)

        def chunk_y(q):
            value = None
            for i in range(NZH * NC):
                w = a_ref.shape[3]
                term = dot_nn(gram[:, i * w : (i + 1) * w], a_ref[i // NC, i % NC, q])
                value = term if value is None else value + term
            ykeep[...] = value

        run(ring_scatter(place, sems, "y", chunk_y, red.at[0], ykeep, *[ybuf.at[step, i] for i in range(6)]))
        if step == 0:
            f = jnp.tile(inv[0:1], (1, xo.shape[1] // 128))
            xo[...] = (1.5 * xo[...] - 0.5 * (red[0] * (f * f))) * f
        else:
            xo[...] = math.sqrt(width) * (1.5 * xo[...] - 0.5 * red[0])
    s = sems.take()
    mine = pl.ds(pl.multiple_of(place.zh * block, block), block)
    theirs = pl.ds(pl.multiple_of((1 - place.zh) * block, block), block)
    last_out[...] = xo[:, theirs].astype(last_out.dtype)
    swap = sems.copy(last_out, last_in, s, place.at(dz=4))
    swap.start()
    out[place.zh] = xo[:, mine]
    swap.wait()
    out[1 - place.zh] = last_in[...].astype(F32)


def shards(embeddings, rotation, codes, codebooks):
    tok_rows, width = embeddings.shape
    cols = rotation.shape[1]
    rows_total = tok_rows * lax.axis_size("dp")
    block = width // lax.axis_size("dp")
    rotated = jnp.dot(embeddings, rotation, preferred_element_type=jnp.float32)
    rebuilt = rebuild_rows(codes, codebooks)
    rebuilt_wide = rebuilt.astype(jnp.float32)
    residue = rotated - rebuilt_wide
    row_error = lax.psum(jnp.sum(residue * residue, axis=1), "col")
    weights = 1.0 / (1.0 + row_error / (2.0 * width))
    weighted_t = (weights[:, None] * rebuilt_wide).astype(BF).T
    place = Place()
    panels = rotation.reshape(NX, NZH, NY, block, NZH, cols // NZH)
    prior = lax.dynamic_index_in_dim(panels, place.x, 0, keepdims=False)
    prior = lax.dynamic_index_in_dim(prior, place.y, 1, keepdims=False)
    prior = lax.dynamic_index_in_dim(prior, place.zh, 2, keepdims=False)
    n = cols // NZH
    m = NZH * block
    prior = prior.reshape(m, n).T.astype(F32)
    panel = m * NY
    wide = n * NZH * NC
    vm = pltpu.VMEM
    out_t = pl.pallas_call(
        functools.partial(main_kernel, 0.2 * rows_total, width),
        out_shape=jax.ShapeDtypeStruct((NZH, n, block), F32),
        in_specs=[pl.BlockSpec(memory_space=pltpu.VMEM)] * 3,
        out_specs=pl.BlockSpec(memory_space=pltpu.VMEM),
        scratch_shapes=[
            vm((n, panel), F32), vm((n, panel), F32),
            vm((2, 6, n, panel), BF), vm((2, 6, n, m), BF),
            vm((n, panel), F32), vm((n, panel), F32),
            vm((2, n, m), F32), vm((n, m), BF), vm((n, m), BF),
            vm((n, m), F32), vm((2, n, m), F32),
            vm((2, NY, n, m), BF), vm((2, NZH, NC, NY, n, m), BF),
            vm((2, n, wide), F32), vm((2, 6, n // NX, wide), BF), vm((n // NX, wide), F32),
            vm((2, NX, n // NX, wide), BF),
            vm((n, m), F32), vm((2, 6, n, m), BF),
            vm((4, 8, 128), F32), vm((4, 7, 8, 128), F32),
            vm((n, block), BF), vm((n, block), BF),
            pltpu.SemaphoreType.DMA((NSEM,)), pltpu.SemaphoreType.DMA((NSEM,)),
        ],
        compiler_params=pltpu.CompilerParams(collective_id=0, has_side_effects=True, vmem_limit_bytes=60 * 2**20),
        name="main",
    )(weighted_t, embeddings, prior)
    return out_t.reshape(cols, block).T


def solution(mesh):
    placed = (P("dp", None), P(None, "col"), P("dp", "col"), P("col", None, None))
    return jax.shard_map(
        shards, mesh=mesh, in_specs=placed, out_specs=P("dp", "col"), check_vma=False
    )
```

```python
import functools
import math

import jax
import jax.numpy as jnp
from jax import lax
from jax.experimental import pallas as pl
from jax.experimental.pallas import tpu as pltpu
from jax.sharding import PartitionSpec as P

MESH = pl.DeviceIdType.MESH
BF = jnp.bfloat16
F32 = jnp.float32
NX, NY, NZH, NZL, NC = 4, 4, 2, 4, 2
NSEM = 480


def rebuild_kernel(codes, table, out):
    lanes = 128

    def one_subspace(m, carry):
        entries = table[m].astype(F32)
        ids = codes[pl.ds(m, 1), :]
        for first in range(0, codes.shape[1], lanes):
            index = jnp.broadcast_to(ids[:, first : first + lanes], (entries.shape[0], lanes))
            within = index % lanes
            value = None
            for part in range(entries.shape[1] // lanes):
                picked = jnp.take_along_axis(
                    entries[:, part * lanes : (part + 1) * lanes], within, axis=1, mode="promise_in_bounds"
                )
                value = picked if value is None else jnp.where(index >= part * lanes, picked, value)
            out[m, :, first : first + lanes] = value
        return carry

    lax.fori_loop(0, codes.shape[0], one_subspace, 0, unroll=4)


def dot_nt(a, b):
    return lax.dot_general(a, b, (((1,), (1,)), ((), ())), preferred_element_type=F32)


def dot_nn(a, b):
    return jnp.dot(a, b, preferred_element_type=F32)


class Place:
    def __init__(self):
        dp, col = lax.axis_index("dp"), lax.axis_index("col")
        self.x = dp // (NZH * NY)
        self.zh = (dp // NY) % NZH
        self.y = dp % NY
        self.zl = col // NC
        self.c = col % NC
        self.z = self.zh * NZL + self.zl

    def at(self, dx=0, dy=0, dz=0, dc=0):
        x = (self.x + dx) % NX
        y = (self.y + dy) % NY
        z = (self.z + dz) % (NZH * NZL)
        c = (self.c + dc) % NC
        return (x * (NZH * NY) + (z // NZL) * NY + y, (z % NZL) * NC + c)

    def col_peer(self, i):
        return (lax.axis_index("dp"), (lax.axis_index("col") + i) % (NZL * NC))

    def other_end(self, i):
        zl = (self.zl + i) % NZL
        return (self.x * (NZH * NY) + (1 - self.zh) * NY + self.y, zl * NC + self.c)

    def along(self, axis, step):
        return self.at(dx=step) if axis == "x" else self.at(dy=step)

    def index(self, axis):
        return self.x if axis == "x" else self.y


class Sems:
    def __init__(self, send, recv):
        self.send, self.recv, self.used = send, recv, 0

    def take(self, count=1):
        base = self.used
        self.used += count
        assert self.used <= NSEM
        return base

    def copy(self, src, dst, index, device):
        return pltpu.make_async_remote_copy(
            src_ref=src,
            dst_ref=dst,
            send_sem=self.send.at[index],
            recv_sem=self.recv.at[index],
            device_id=device,
            device_id_type=MESH,
        )


def ring_scatter(place, sems, axis, chunk, out, keep, diag, got, to_r, to_l, from_l, from_r):
    rows = diag.shape[0]
    half = rows // 2
    lo, hi = pl.ds(0, half), pl.ds(half, half)
    p = place.index(axis)
    right, left = place.along(axis, 1), place.along(axis, -1)
    s = sems.take(6)
    chunk((p + 2) % 4)
    diag[...] = keep[...].astype(BF)
    c0 = sems.copy(diag.at[lo], got.at[lo], s, right)
    c1 = sems.copy(diag.at[hi], got.at[hi], s + 1, left)
    c0.start()
    c1.start()
    yield
    chunk((p + 1) % 4)
    to_r[hi] = keep[hi].astype(BF)
    c2 = sems.copy(to_r.at[hi], from_l.at[hi], s + 2, right)
    c2.start()
    c0.wait_recv()
    to_r[lo] = (keep[lo] + got[lo].astype(F32)).astype(BF)
    c3 = sems.copy(to_r.at[lo], from_l.at[lo], s + 3, right)
    c3.start()
    yield
    chunk((p + 3) % 4)
    to_l[lo] = keep[lo].astype(BF)
    c4 = sems.copy(to_l.at[lo], from_r.at[lo], s + 4, left)
    c4.start()
    c1.wait_recv()
    to_l[hi] = (keep[hi] + got[hi].astype(F32)).astype(BF)
    c5 = sems.copy(to_l.at[hi], from_r.at[hi], s + 5, left)
    c5.start()
    yield
    chunk(p)
    for c in (c2, c3, c4, c5):
        c.wait_recv()
    out[...] = keep[...] + from_l[...].astype(F32) + from_r[...].astype(F32)
    for c in (c0, c1, c2, c3, c4, c5):
        c.wait_send()


def ring_gather(place, sems, axis, buf, first=0, rows=None):
    rows = buf.shape[1] if rows is None else rows
    half = rows // 2
    all_rows, lo, hi = pl.ds(first, rows), pl.ds(first, half), pl.ds(first + half, half)
    p = place.index(axis)
    right, left = place.along(axis, 1), place.along(axis, -1)
    s = sems.take(4)
    before, after = (p + 3) % 4, (p + 1) % 4
    c0 = sems.copy(buf.at[p, all_rows], buf.at[p, all_rows], s, right)
    c1 = sems.copy(buf.at[p, all_rows], buf.at[p, all_rows], s + 1, left)
    c0.start()
    c1.start()
    yield
    c0.wait_recv()
    c2 = sems.copy(buf.at[before, lo], buf.at[before, lo], s + 2, right)
    c2.start()
    c1.wait_recv()
    c3 = sems.copy(buf.at[after, hi], buf.at[after, hi], s + 3, left)
    c3.start()
    yield
    c2.wait_recv()
    c3.wait_recv()
    for c in (c0, c1, c2, c3):
        c.wait_send()


def run(*gens):
    live = list(gens)
    while live:
        pump(live)


def pump(live):
    for g in list(live):
        if next(g, live) is live:
            live.remove(g)


class Spread:
    def __init__(self, place, sems, bt, at):
        self.place, self.sems, self.bt, self.at = place, sems, bt, at
        z = place.z
        self.d = (place.zl - place.y + 4) % 4
        self.back = (4 - self.d) % 4
        self.up, self.down, self.other = place.at(dz=1), place.at(dz=-1), place.at(dc=1)
        self.up_origin = ((z - self.d + 8) % 8) // 4
        self.down_origin = ((z + self.back) % 8) // 4
        self.parts, self.slots = at.shape[0], at.shape[1]
        self.rows = at.shape[4]
        self.count = self.parts * self.slots
        n = self.count
        self.s_up, self.s_down = sems.take(n), sems.take(n)
        self.s_up_half, self.s_down_half = sems.take(n), sems.take(n)
        self.s_core = sems.take(2 * n)

    def spot(self, origin, n, part=None):
        ref = self.at.at[n // self.slots, n % self.slots, origin, self.place.c]
        half = self.rows // 2
        if part is not None:
            ref = ref.at[pl.ds(part * half, half)]
        return ref

    def source(self, n):
        first = pl.multiple_of((n // self.slots) * self.rows, self.rows)
        return self.bt.at[n % self.slots, pl.ds(first, self.rows)]

    def full(self, up, n, from_source=False):
        origin = self.up_origin if up else self.down_origin
        src = self.source(n) if from_source else self.spot(origin, n)
        base, device = (self.s_up, self.up) if up else (self.s_down, self.down)
        return self.sems.copy(src, self.spot(origin, n), base + n, device)

    def half(self, up, n, origin):
        part = 0 if up else 1
        base, device = (self.s_up_half, self.up) if up else (self.s_down_half, self.down)
        return self.sems.copy(self.spot(origin, n, part), self.spot(origin, n, part), base + n, device)

    def core(self, origin, n, from_source=False):
        src = self.source(n) if from_source else self.spot(origin, n)
        return self.sems.copy(src, self.spot(origin, n), self.s_core + origin * self.count + n, self.other)

    def steps(self, first, last):
        d, n_all, far = self.d, self.count, 1 - self.place.zh

        def slot(t, carry):
            @pl.when((d == 0) & (t < n_all))
            def _():
                self.full(True, t, True).start()
                self.full(False, t, True).start()
                self.core(self.place.zh, t, True).start()

            for up, lag, last_d in ((True, d, 3), (False, self.back, 1)):
                origin = self.up_origin if up else self.down_origin
                n = t - lag

                @pl.when((d > 0) & (n >= 0) & (n < n_all))
                def _(up=up, n=n, last_d=last_d, origin=origin):
                    self.full(up, n).wait_recv()

                    @pl.when(d != last_d)
                    def _():
                        self.full(up, n).start()

                    @pl.when(d == last_d)
                    def _():
                        self.half(up, n, origin).start()

                    self.core(origin, n).start()

            n = t - 4

            @pl.when((d == 0) & (n >= 0))
            def _():
                self.half(True, n, far).wait_recv()
                self.half(False, n, far).wait_recv()
                self.core(far, n).start()

            return carry

        lax.fori_loop(first, last, slot, 0)

    def arrived(self, r):
        for q in range(self.slots):
            for origin in range(2):
                self.core(origin, r * self.slots + q).wait_recv()

        @pl.when(self.d == 0)
        def _():
            for q in range(self.slots):
                rows = pl.ds(r * self.rows, self.rows)
                self.at[r, q, self.place.zh, self.place.c] = self.bt[q, rows]

    def sent(self):
        d = self.d

        def one(n, carry):
            for up, last_d in ((True, 3), (False, 1)):
                origin = self.up_origin if up else self.down_origin

                @pl.when(d != last_d)
                def _(up=up):
                    self.full(up, n).wait_send()

                @pl.when(d == last_d)
                def _(up=up, origin=origin):
                    self.half(up, n, origin).wait_send()

            for origin in range(2):
                self.core(origin, n).wait_send()
            return carry

        lax.fori_loop(0, self.count, one, 0)


def share_sum(place, sems, mine, slots, partners):
    s = sems.take(len(partners))
    copies = [sems.copy(mine, slots.at[i], s + i, device) for i, device in enumerate(partners)]
    for c in copies:
        c.start()
    return copies


def finish_sum(copies, mine, slots):
    for c in copies:
        c.wait()
    total = mine[...]
    for i in range(len(copies)):
        total = total + slots[i]
    return total


def main_kernel(
    prior_scale, width, rebuilt, e, rot, out,
    wt, err, err_in, keep_a, keep_b, big, small, own_a, own_b, ab, ab_out, ab_in, xo, red,
    bt, at, gkeep, gtake, gbuf, gown, gfull, ykeep, ybuf, sq, sq_in, last_out, last_in,
    send, recv,
):
    place = Place()
    sems = Sems(send, recv)
    barrier = pltpu.get_barrier_semaphore()
    col_peers = [place.col_peer(i) for i in range(1, NZL * NC)]
    partners = (
        [place.at(dx=i) for i in (1, 2, 3)]
        + [place.at(dy=i) for i in (1, 2, 3)]
        + [place.other_end(i) for i in range(NZL)]
        + col_peers
    )
    for device in partners:
        pl.semaphore_signal(barrier, inc=1, device_id=device, device_id_type=MESH)

    tok_rows = e.shape[0]
    step_rows = tok_rows // 2
    for first in range(0, tok_rows, step_rows):
        rotated = dot_nn(e[first : first + step_rows], rot[...])
        residue = rotated.T - rebuilt[:, first : first + step_rows]
        squares = residue * residue
        err[:, first : first + step_rows] = jnp.sum(squares.reshape(squares.shape[0] // 8, 8, step_rows), axis=0)
    pl.semaphore_wait(barrier, len(partners))

    total = jnp.sum(finish_sum(share_sum(place, sems, err, err_in, col_peers), err, err_in), axis=0, keepdims=True)
    weights = 1.0 / (1.0 + total / (2.0 * width))
    wt[...] = (rebuilt[...] * weights).astype(BF)

    block = out.shape[2]
    n_half = wt.shape[0] // 2
    x_cols = e.shape[1] // NX

    def chunk_a(xi):
        start = pl.multiple_of(xi * x_cols, x_cols)
        value = dot_nn(wt[0:n_half], e[:, pl.ds(start, x_cols)])
        for zh in range(NZH):
            for y in range(NY):
                at_in, at_out = (zh * NY + y) * block, (y * NZH + zh) * block
                keep_a[:, at_out : at_out + block] = value[:, at_in : at_in + block]

    def chunk_b(yi):
        parts = []
        for x in range(NX):
            for zh in range(NZH):
                start = pl.multiple_of(x * x_cols + (zh * NY + yi) * block, block)
                parts.append(e[:, pl.ds(start, block)])
        keep_b[...] = dot_nn(wt[n_half:], jnp.concatenate(parts, axis=1))

    def piece(source, keep):
        def chunk(i):
            width_of = keep.shape[1]
            keep[...] = source[:, pl.ds(pl.multiple_of(i * width_of, width_of), width_of)]

        return chunk

    run(
        ring_scatter(place, sems, "x", chunk_a, own_a, keep_a, *[big.at[0, i] for i in range(6)]),
        ring_scatter(place, sems, "y", chunk_b, own_b, keep_b, *[big.at[1, i] for i in range(6)]),
    )
    run(
        ring_scatter(place, sems, "y", piece(own_a, red.at[0]), ab.at[0], red.at[0], *[small.at[0, i] for i in range(6)]),
        ring_scatter(place, sems, "x", piece(own_b, red.at[1]), ab.at[1], red.at[1], *[small.at[1, i] for i in range(6)]),
    )
    ab_out[...] = ab[1 - place.zh].astype(BF)
    s = sems.take()
    swap = sems.copy(ab_out, ab_in, s, place.at(dz=4))
    swap.start()
    for zh in range(NZH):
        rows = pl.ds(pl.multiple_of(place.x * x_cols + (zh * NY + place.y) * block, block), block)
        cols = pl.ds(pl.multiple_of(place.zh * n_half, n_half), n_half)
        xo[:, zh * block : (zh + 1) * block] = prior_scale * rot[rows, cols].astype(F32).T
    swap.wait()
    x_new = ab[place.zh] + ab_in[...].astype(F32) + xo[...]
    xo[...] = x_new
    squares = x_new * x_new
    folded = jnp.sum(squares.reshape(squares.shape[0] // 8, 8, squares.shape[1]), axis=0)
    part = folded[:, 0:128]
    for i in range(1, folded.shape[1] // 128):
        part = part + folded[:, i * 128 : (i + 1) * 128]
    sq[0] = part

    y_copies = share_sum(place, sems, sq.at[0], sq_in.at[0], [place.at(dy=i) for i in (1, 2, 3)])
    inv = None
    for step in range(2):
        b_ref, a_ref, g_ref = bt.at[step], at.at[step], gfull.at[step]
        parts, rows = a_ref.shape[0], a_ref.shape[4]
        wide = NZH * NC * rows
        b_ref[place.y] = xo[...].astype(BF)
        panel = [ring_gather(place, sems, "y", b_ref, r * rows, rows) for r in range(parts)]
        for g in panel:
            next(g)
        spread = Spread(place, sems, b_ref, a_ref)

        def reduce_gram(r):
            total = None
            for q in range(NY):
                term = dot_nt(b_ref[q], a_ref[r, q].reshape(wide, a_ref.shape[5]))
                total = term if total is None else total + term
            gkeep[r] = total
            g_rows = total.shape[0] // NX

            def chunk_g(xi):
                gtake[r] = gkeep[r, pl.ds(pl.multiple_of(xi * g_rows, g_rows), g_rows)]

            yield from ring_scatter(
                place, sems, "x", chunk_g, gown.at[r], gtake.at[r], *[gbuf.at[step, r, i] for i in range(6)]
            )
            g_ref[r, place.x] = gown[r].astype(BF)
            yield from ring_gather(place, sems, "x", g_ref.at[r])

        grams = []
        done = 0
        for seg in range(parts + 1):
            need = parts if seg > 1 else seg + 1
            while done < min(need, parts):
                run(panel[done])
                done += 1
            spread.steps(seg * spread.slots, (seg + 1) * spread.slots)
            if seg > 0:
                if done < parts:
                    run(*panel[done:])
                    done = parts
                spread.arrived(seg - 1)
                pump(grams)
                g = reduce_gram(seg - 1)
                next(g)
                grams.append(g)
            if step == 0 and seg == 1:
                sq[1] = finish_sum(y_copies, sq.at[0], sq_in.at[0])
                z_copies = share_sum(place, sems, sq.at[1], sq_in.at[1], [place.at(dz=i) for i in range(1, 8)])
            if step == 0 and seg == 3:
                sq[2] = finish_sum(z_copies, sq.at[1], sq_in.at[1])
                c_copies = share_sum(place, sems, sq.at[2], sq_in.at[2], [place.at(dc=1)])
        if step == 0:
            sq[3] = finish_sum(c_copies, sq.at[2], sq_in.at[2])
            x_copies = share_sum(place, sems, sq.at[3], sq_in.at[3], [place.at(dx=i) for i in (1, 2, 3)])
        run(*grams)
        if step == 0:
            total = jnp.sum(finish_sum(x_copies, sq.at[3], sq_in.at[3]))
            scale2 = jnp.full((8, 128), 1.96 / width, F32) * total
            inv = 1.0 / jnp.sqrt(scale2)

        def chunk_y(q):
            value = None
            for r in range(parts):
                gram = jnp.concatenate([g_ref[r, i] for i in range(NX)], axis=0)
                term = dot_nn(gram, a_ref[r, q].reshape(wide, a_ref.shape[5]))
                value = term if value is None else value + term
            ykeep[...] = value

        run(ring_scatter(place, sems, "y", chunk_y, red.at[0], ykeep, *[ybuf.at[step, i] for i in range(6)]))
        if step == 0:
            f = jnp.tile(inv[0:1], (1, xo.shape[1] // 128))
            xo[...] = (1.5 * xo[...] - 0.5 * (red[0] * (f * f))) * f
        else:
            xo[...] = math.sqrt(width) * (1.5 * xo[...] - 0.5 * red[0])
        spread.sent()
    s = sems.take()
    mine = pl.ds(pl.multiple_of(place.zh * block, block), block)
    theirs = pl.ds(pl.multiple_of((1 - place.zh) * block, block), block)
    last_out[...] = xo[:, theirs].astype(last_out.dtype)
    swap = sems.copy(last_out, last_in, s, place.at(dz=4))
    swap.start()
    out[place.zh] = xo[:, mine]
    swap.wait()
    out[1 - place.zh] = last_in[...].astype(F32)


def shards(embeddings, rotation, codes, codebooks):
    tok_rows, width = embeddings.shape
    cols = rotation.shape[1]
    subs, centroids, sub_width = codebooks.shape
    rows_total = tok_rows * lax.axis_size("dp")
    block = width // lax.axis_size("dp")
    rebuilt = pl.pallas_call(
        rebuild_kernel,
        out_shape=jax.ShapeDtypeStruct((subs, sub_width, tok_rows), F32),
        in_specs=[pl.BlockSpec(memory_space=pltpu.VMEM)] * 2,
        out_specs=pl.BlockSpec(memory_space=pltpu.VMEM),
        name="rebuild",
    )(codes.T, codebooks.transpose(0, 2, 1)).reshape(cols, tok_rows)
    n = cols // NZH
    m = NZH * block
    panel = m * NY
    parts = 4
    rows = n // parts
    wide = NZH * NC * rows
    vm = pltpu.VMEM
    out_t = pl.pallas_call(
        functools.partial(main_kernel, 0.2 * rows_total, width),
        out_shape=jax.ShapeDtypeStruct((NZH, n, block), F32),
        in_specs=[pl.BlockSpec(memory_space=pltpu.VMEM)] * 3,
        out_specs=pl.BlockSpec(memory_space=pltpu.VMEM),
        scratch_shapes=[
            vm((cols, tok_rows), BF), vm((8, tok_rows), F32), vm((NZL * NC - 1, 8, tok_rows), F32),
            vm((n, panel), F32), vm((n, panel), F32),
            vm((2, 6, n, panel), BF), vm((2, 6, n, m), BF),
            vm((n, panel), F32), vm((n, panel), F32),
            vm((2, n, m), F32), vm((n, m), BF), vm((n, m), BF),
            vm((n, m), F32), vm((2, n, m), F32),
            vm((2, NY, n, m), BF), vm((2, parts, NY, NZH, NC, rows, m), BF),
            vm((parts, n, wide), F32), vm((parts, n // NX, wide), F32),
            vm((2, parts, 6, n // NX, wide), BF), vm((parts, n // NX, wide), F32),
            vm((2, parts, NX, n // NX, wide), BF),
            vm((n, m), F32), vm((2, 6, n, m), BF),
            vm((4, 8, 128), F32), vm((4, 7, 8, 128), F32),
            vm((n, block), BF), vm((n, block), BF),
            pltpu.SemaphoreType.DMA((NSEM,)), pltpu.SemaphoreType.DMA((NSEM,)),
        ],
        compiler_params=pltpu.CompilerParams(collective_id=0, has_side_effects=True, vmem_limit_bytes=60 * 2**20),
        name="main",
    )(rebuilt, embeddings, rotation)
    return out_t.reshape(cols, block).T


def solution(mesh):
    placed = (P("dp", None), P(None, "col"), P("dp", "col"), P("col", None, None))
    return jax.shard_map(
        shards, mesh=mesh, in_specs=placed, out_specs=P("dp", "col"), check_vma=False
    )
```

```python
import functools
import math

import jax
import jax.numpy as jnp
from jax import lax
from jax.experimental import pallas as pl
from jax.experimental.pallas import tpu as pltpu
from jax.sharding import PartitionSpec as P

MESH = pl.DeviceIdType.MESH
BF = jnp.bfloat16
F32 = jnp.float32
NX, NY, NZH, NZL, NC = 4, 4, 2, 4, 2
NSEM = 480
LAG = 3
PARTS = 4
PAIR = 2


def rebuild_kernel(codes, table, out):
    lanes = 128

    def one_subspace(m, carry):
        entries = table[m].astype(F32)
        ids = codes[pl.ds(m, 1), :]
        for first in range(0, codes.shape[1], lanes):
            index = jnp.broadcast_to(ids[:, first : first + lanes], (entries.shape[0], lanes))
            within = index % lanes
            value = None
            for part in range(entries.shape[1] // lanes):
                picked = jnp.take_along_axis(
                    entries[:, part * lanes : (part + 1) * lanes], within, axis=1, mode="promise_in_bounds"
                )
                value = picked if value is None else jnp.where(index >= part * lanes, picked, value)
            out[m, :, first : first + lanes] = value
        return carry

    lax.fori_loop(0, codes.shape[0], one_subspace, 0, unroll=4)


def dot_nt(a, b):
    return lax.dot_general(a, b, (((1,), (1,)), ((), ())), preferred_element_type=F32)


def dot_nn(a, b):
    return jnp.dot(a, b, preferred_element_type=F32)


class Place:
    def __init__(self):
        dp, col = lax.axis_index("dp"), lax.axis_index("col")
        self.x = dp // (NZH * NY)
        self.zh = (dp // NY) % NZH
        self.y = dp % NY
        self.zl = col // NC
        self.c = col % NC
        self.z = self.zh * NZL + self.zl

    def at(self, dx=0, dy=0, dz=0, dc=0):
        x = (self.x + dx) % NX
        y = (self.y + dy) % NY
        z = (self.z + dz) % (NZH * NZL)
        c = (self.c + dc) % NC
        return (x * (NZH * NY) + (z // NZL) * NY + y, (z % NZL) * NC + c)

    def col_peer(self, i):
        return (lax.axis_index("dp"), (lax.axis_index("col") + i) % (NZL * NC))

    def other_end(self, i):
        zl = (self.zl + i) % NZL
        return (self.x * (NZH * NY) + (1 - self.zh) * NY + self.y, zl * NC + self.c)

    def along(self, axis, step):
        return self.at(dx=step) if axis == "x" else self.at(dy=step)

    def index(self, axis):
        return self.x if axis == "x" else self.y


class Sems:
    def __init__(self, send, recv):
        self.send, self.recv, self.used = send, recv, 0

    def take(self, count=1):
        base = self.used
        self.used += count
        assert self.used <= NSEM
        return base

    def copy(self, src, dst, index, device):
        return pltpu.make_async_remote_copy(
            src_ref=src,
            dst_ref=dst,
            send_sem=self.send.at[index],
            recv_sem=self.recv.at[index],
            device_id=device,
            device_id_type=MESH,
        )


def ring_scatter(place, sems, axis, chunk, out, keep, diag, got, to_r, to_l, from_l, from_r):
    rows = diag.shape[0]
    half = rows // 2
    lo, hi = pl.ds(0, half), pl.ds(half, half)
    p = place.index(axis)
    right, left = place.along(axis, 1), place.along(axis, -1)
    s = sems.take(6)
    chunk((p + 2) % 4)
    diag[...] = keep[...].astype(BF)
    c0 = sems.copy(diag.at[lo], got.at[lo], s, right)
    c1 = sems.copy(diag.at[hi], got.at[hi], s + 1, left)
    c0.start()
    c1.start()
    yield
    chunk((p + 1) % 4)
    to_r[hi] = keep[hi].astype(BF)
    c2 = sems.copy(to_r.at[hi], from_l.at[hi], s + 2, right)
    c2.start()
    c0.wait_recv()
    to_r[lo] = (keep[lo] + got[lo].astype(F32)).astype(BF)
    c3 = sems.copy(to_r.at[lo], from_l.at[lo], s + 3, right)
    c3.start()
    yield
    chunk((p + 3) % 4)
    to_l[lo] = keep[lo].astype(BF)
    c4 = sems.copy(to_l.at[lo], from_r.at[lo], s + 4, left)
    c4.start()
    c1.wait_recv()
    to_l[hi] = (keep[hi] + got[hi].astype(F32)).astype(BF)
    c5 = sems.copy(to_l.at[hi], from_r.at[hi], s + 5, left)
    c5.start()
    yield
    chunk(p)
    for c in (c2, c3, c4, c5):
        c.wait_recv()
    out[...] = keep[...] + from_l[...].astype(F32) + from_r[...].astype(F32)
    for c in (c0, c1, c2, c3, c4, c5):
        c.wait_send()


def ring_gather(place, sems, axis, buf, first=0, rows=None):
    rows = buf.shape[1] if rows is None else rows
    half = rows // 2
    all_rows, lo, hi = pl.ds(first, rows), pl.ds(first, half), pl.ds(first + half, half)
    p = place.index(axis)
    right, left = place.along(axis, 1), place.along(axis, -1)
    s = sems.take(4)
    before, after = (p + 3) % 4, (p + 1) % 4
    c0 = sems.copy(buf.at[p, all_rows], buf.at[p, all_rows], s, right)
    c1 = sems.copy(buf.at[p, all_rows], buf.at[p, all_rows], s + 1, left)
    c0.start()
    c1.start()
    yield
    c0.wait_recv()
    c2 = sems.copy(buf.at[before, lo], buf.at[before, lo], s + 2, right)
    c2.start()
    c1.wait_recv()
    c3 = sems.copy(buf.at[after, hi], buf.at[after, hi], s + 3, left)
    c3.start()
    yield
    c2.wait_recv()
    c3.wait_recv()
    for c in (c0, c1, c2, c3):
        c.wait_send()


def run(*gens):
    live = list(gens)
    while live:
        pump(live)


def pump(live):
    for g in list(live):
        if next(g, live) is live:
            live.remove(g)


class Spread:
    def __init__(self, place, sems, bt, at):
        self.place, self.sems, self.bt, self.at = place, sems, bt, at
        z = place.z
        self.d = (place.zl - place.y + 4) % 4
        self.back = (4 - self.d) % 4
        self.up, self.down, self.other = place.at(dz=1), place.at(dz=-1), place.at(dc=1)
        self.up_origin = ((z - self.d + 8) % 8) // 4
        self.down_origin = ((z + self.back) % 8) // 4
        self.parts, self.slots = at.shape[0], at.shape[1] // PAIR
        self.rows = at.shape[4]
        self.count = self.parts * self.slots
        n = self.count
        self.s_up, self.s_down = sems.take(n), sems.take(n)
        self.s_up_half, self.s_down_half = sems.take(n), sems.take(n)
        self.s_core = sems.take(2 * n)

    def spot(self, origin, n, part=None):
        blocks = pl.ds((n % self.slots) * PAIR, PAIR)
        half = self.rows // 2
        rows = pl.ds(0, self.rows) if part is None else pl.ds(part * half, half)
        return self.at.at[n // self.slots, blocks, origin, self.place.c, rows]

    def source(self, n):
        first = pl.multiple_of((n // self.slots) * self.rows, self.rows)
        return self.bt.at[pl.ds((n % self.slots) * PAIR, PAIR), pl.ds(first, self.rows)]

    def full(self, up, n, from_source=False):
        origin = self.up_origin if up else self.down_origin
        src = self.source(n) if from_source else self.spot(origin, n)
        base, device = (self.s_up, self.up) if up else (self.s_down, self.down)
        return self.sems.copy(src, self.spot(origin, n), base + n, device)

    def half(self, up, n, origin):
        part = 0 if up else 1
        base, device = (self.s_up_half, self.up) if up else (self.s_down_half, self.down)
        return self.sems.copy(self.spot(origin, n, part), self.spot(origin, n, part), base + n, device)

    def core(self, origin, n, from_source=False):
        src = self.source(n) if from_source else self.spot(origin, n)
        return self.sems.copy(src, self.spot(origin, n), self.s_core + origin * self.count + n, self.other)

    def steps(self, first, last, after=None):
        d, n_all, far = self.d, self.count, 1 - self.place.zh

        def slot(t, carry):
            @pl.when((d == 0) & (t < n_all))
            def _():
                self.full(True, t, True).start()
                self.full(False, t, True).start()
                self.core(self.place.zh, t, True).start()

            for up, lag, last_d in ((True, d, 3), (False, self.back, 1)):
                origin = self.up_origin if up else self.down_origin
                n = t - LAG * lag

                @pl.when((d > 0) & (n >= 0) & (n < n_all))
                def _(up=up, n=n, last_d=last_d, origin=origin):
                    self.full(up, n).wait_recv()

                    @pl.when(d != last_d)
                    def _():
                        self.full(up, n).start()

                    @pl.when(d == last_d)
                    def _():
                        self.half(up, n, origin).start()

                    self.core(origin, n).start()

            n = t - LAG * 4

            @pl.when((d == 0) & (n >= 0) & (n < n_all))
            def _():
                self.half(True, n, far).wait_recv()
                self.half(False, n, far).wait_recv()
                self.core(far, n).start()

            if after is not None:
                after(t)
            return carry

        lax.fori_loop(first, last, slot, 0)

    def arrived(self, r):
        for q in range(self.slots):
            for origin in range(2):
                self.core(origin, r * self.slots + q).wait_recv()

        @pl.when(self.d == 0)
        def _():
            for q in range(self.slots * PAIR):
                rows = pl.ds(pl.multiple_of(r * self.rows, self.rows), self.rows)
                self.at[r, q, self.place.zh, self.place.c] = self.bt[q, rows]

    def sent(self):
        d = self.d

        def one(n, carry):
            for up, last_d in ((True, 3), (False, 1)):
                origin = self.up_origin if up else self.down_origin

                @pl.when(d != last_d)
                def _(up=up):
                    self.full(up, n).wait_send()

                @pl.when(d == last_d)
                def _(up=up, origin=origin):
                    self.half(up, n, origin).wait_send()

            for origin in range(2):
                self.core(origin, n).wait_send()
            return carry

        lax.fori_loop(0, self.count, one, 0)


class GramReduce:
    def __init__(self, place, sems, spread, keep, bufs, full):
        self.place, self.sems, self.spread = place, sems, spread
        self.keep, self.bufs, self.full = keep, bufs, full
        self.s = sems.take(10 * full.shape[0])
        self.right, self.left = place.at(dx=1), place.at(dx=-1)
        self.rows = full.shape[2]
        self.half = self.rows // 2
        self.lo, self.hi = pl.ds(0, self.half), pl.ds(self.half, self.half)

    def sc(self, r, i):
        diag, got, to_r, to_l, from_l, from_r = [self.bufs.at[r, k] for k in range(6)]
        src, dst, part, device = (
            (diag, got, self.lo, self.right),
            (diag, got, self.hi, self.left),
            (to_r, from_l, self.hi, self.right),
            (to_r, from_l, self.lo, self.right),
            (to_l, from_r, self.lo, self.left),
            (to_l, from_r, self.hi, self.left),
        )[i]
        return self.sems.copy(src.at[part], dst.at[part], self.s + 10 * r + i, device)

    def ga(self, r, i):
        x = self.place.x
        slot, part, device = (
            (x, pl.ds(0, self.rows), self.right),
            (x, pl.ds(0, self.rows), self.left),
            ((x + 3) % 4, self.lo, self.right),
            ((x + 1) % 4, self.hi, self.left),
        )[i]
        ref = self.full.at[r, slot, part]
        return self.sems.copy(ref, ref, self.s + 10 * r + 6 + i, device)

    def mine(self, r, i, part):
        first = i * self.rows + part * self.half
        return self.keep[r, pl.ds(pl.multiple_of(first, self.half), self.half)]

    def stage(self, number, r):
        x = self.place.x
        if number == 0:
            self.spread.arrived(r)
            bt, at = self.spread.bt, self.spread.at
            wide = at.shape[2] * at.shape[3] * at.shape[4]
            total = None
            for q in range(at.shape[1]):
                term = dot_nt(bt[q], at[r, q].reshape(wide, at.shape[5]))
                total = term if total is None else total + term
            self.keep[r] = total
            for part, rows in ((0, self.lo), (1, self.hi)):
                self.bufs[r, 0, rows] = self.mine(r, (x + 2) % 4, part).astype(BF)
            self.sc(r, 0).start()
            self.sc(r, 1).start()
            self.bufs[r, 2, self.hi] = self.mine(r, (x + 1) % 4, 1).astype(BF)
            self.sc(r, 2).start()
            self.bufs[r, 3, self.lo] = self.mine(r, (x + 3) % 4, 0).astype(BF)
            self.sc(r, 4).start()
        elif number == 1:
            self.sc(r, 0).wait_recv()
            got = self.bufs[r, 1, self.lo].astype(F32)
            self.bufs[r, 2, self.lo] = (self.mine(r, (x + 1) % 4, 0) + got).astype(BF)
            self.sc(r, 3).start()
            self.sc(r, 1).wait_recv()
            got = self.bufs[r, 1, self.hi].astype(F32)
            self.bufs[r, 3, self.hi] = (self.mine(r, (x + 3) % 4, 1) + got).astype(BF)
            self.sc(r, 5).start()
        elif number == 2:
            for i in (2, 3, 4, 5):
                self.sc(r, i).wait_recv()
            for part, rows in ((0, self.lo), (1, self.hi)):
                total = self.mine(r, x, part) + self.bufs[r, 4, rows].astype(F32) + self.bufs[r, 5, rows].astype(F32)
                self.full[r, x, rows] = total.astype(BF)
            self.ga(r, 0).start()
            self.ga(r, 1).start()
        elif number == 3:
            self.ga(r, 0).wait_recv()
            self.ga(r, 2).start()
            self.ga(r, 1).wait_recv()
            self.ga(r, 3).start()
        else:
            self.ga(r, 2).wait_recv()
            self.ga(r, 3).wait_recv()
            for i in range(6):
                self.sc(r, i).wait_send()
            for i in range(4):
                self.ga(r, i).wait_send()


def share_sum(place, sems, mine, slots, partners):
    s = sems.take(len(partners))
    copies = [sems.copy(mine, slots.at[i], s + i, device) for i, device in enumerate(partners)]
    for c in copies:
        c.start()
    return copies


def finish_sum(copies, mine, slots):
    for c in copies:
        c.wait()
    total = mine[...]
    for i in range(len(copies)):
        total = total + slots[i]
    return total


def main_kernel(
    prior_scale, width, rebuilt, e, rot, out,
    wt, err, err_in, keep_a, keep_b, big, small, own_a, own_b, ab, ab_out, ab_in, xo, red,
    bt, at, gkeep, gbuf, gfull, ykeep, ybuf, sq, sq_in, last_out, last_in,
    send, recv,
):
    place = Place()
    sems = Sems(send, recv)
    barrier = pltpu.get_barrier_semaphore()
    col_peers = [place.col_peer(i) for i in range(1, NZL * NC)]
    partners = (
        [place.at(dx=i) for i in (1, 2, 3)]
        + [place.at(dy=i) for i in (1, 2, 3)]
        + [place.other_end(i) for i in range(NZL)]
        + col_peers
    )
    for device in partners:
        pl.semaphore_signal(barrier, inc=1, device_id=device, device_id_type=MESH)

    tok_rows = e.shape[0]
    step_rows = tok_rows // 2
    for first in range(0, tok_rows, step_rows):
        rotated = dot_nn(e[first : first + step_rows], rot[...])
        residue = rotated.T - rebuilt[:, first : first + step_rows]
        squares = residue * residue
        err[:, first : first + step_rows] = jnp.sum(squares.reshape(squares.shape[0] // 8, 8, step_rows), axis=0)
    pl.semaphore_wait(barrier, len(partners))

    total = jnp.sum(finish_sum(share_sum(place, sems, err, err_in, col_peers), err, err_in), axis=0, keepdims=True)
    weights = 1.0 / (1.0 + total / (2.0 * width))
    wt[...] = (rebuilt[...] * weights).astype(BF)

    block = out.shape[2]
    n_half = wt.shape[0] // 2
    x_cols = e.shape[1] // NX

    def chunk_a(xi):
        start = pl.multiple_of(xi * x_cols, x_cols)
        value = dot_nn(wt[0:n_half], e[:, pl.ds(start, x_cols)])
        for zh in range(NZH):
            for y in range(NY):
                at_in, at_out = (zh * NY + y) * block, (y * NZH + zh) * block
                keep_a[:, at_out : at_out + block] = value[:, at_in : at_in + block]

    def chunk_b(yi):
        parts = []
        for x in range(NX):
            for zh in range(NZH):
                start = pl.multiple_of(x * x_cols + (zh * NY + yi) * block, block)
                parts.append(e[:, pl.ds(start, block)])
        keep_b[...] = dot_nn(wt[n_half:], jnp.concatenate(parts, axis=1))

    def piece(source, keep):
        def chunk(i):
            width_of = keep.shape[1]
            keep[...] = source[:, pl.ds(pl.multiple_of(i * width_of, width_of), width_of)]

        return chunk

    run(
        ring_scatter(place, sems, "x", chunk_a, own_a, keep_a, *[big.at[0, i] for i in range(6)]),
        ring_scatter(place, sems, "y", chunk_b, own_b, keep_b, *[big.at[1, i] for i in range(6)]),
    )
    run(
        ring_scatter(place, sems, "y", piece(own_a, red.at[0]), ab.at[0], red.at[0], *[small.at[0, i] for i in range(6)]),
        ring_scatter(place, sems, "x", piece(own_b, red.at[1]), ab.at[1], red.at[1], *[small.at[1, i] for i in range(6)]),
    )
    ab_out[...] = ab[1 - place.zh].astype(BF)
    s = sems.take()
    swap = sems.copy(ab_out, ab_in, s, place.at(dz=4))
    swap.start()
    for zh in range(NZH):
        rows = pl.ds(pl.multiple_of(place.x * x_cols + (zh * NY + place.y) * block, block), block)
        cols = pl.ds(pl.multiple_of(place.zh * n_half, n_half), n_half)
        xo[:, zh * block : (zh + 1) * block] = prior_scale * rot[rows, cols].astype(F32).T
    swap.wait()
    x_new = ab[place.zh] + ab_in[...].astype(F32) + xo[...]
    xo[...] = x_new
    squares = x_new * x_new
    folded = jnp.sum(squares.reshape(squares.shape[0] // 8, 8, squares.shape[1]), axis=0)
    part = folded[:, 0:128]
    for i in range(1, folded.shape[1] // 128):
        part = part + folded[:, i * 128 : (i + 1) * 128]
    sq[0] = part

    y_copies = share_sum(place, sems, sq.at[0], sq_in.at[0], [place.at(dy=i) for i in (1, 2, 3)])
    inv = None
    for step in range(2):
        b_ref, a_ref, g_ref = bt.at[step], at.at[step], gfull.at[step]
        parts, rows = a_ref.shape[0], a_ref.shape[4]
        wide = NZH * NC * rows
        b_ref[place.y] = xo[...].astype(BF)
        panel = [ring_gather(place, sems, "y", b_ref, r * rows, rows) for r in range(parts)]
        for g in panel:
            next(g)
        spread = Spread(place, sems, b_ref, a_ref)
        grams = GramReduce(place, sems, spread, gkeep, gbuf.at[step], g_ref)
        per, gap, stages = spread.slots, spread.slots, 5
        d = spread.d
        hops = 4 - d + (d // 3) * 2

        def after(t):
            for number in reversed(range(stages)):
                ahead = t - gap * number - (per - 1) - LAG * hops

                @pl.when((ahead >= 0) & (ahead % per == 0) & (ahead < per * parts))
                def _(number=number, ahead=ahead):
                    grams.stage(number, ahead // per)

        run(panel[0])
        for g in panel[1:]:
            next(g)
        for r in range(1, parts):
            spread.steps((r - 1) * per, r * per)
            run(panel[r])
        if step == 0:
            sq[1] = finish_sum(y_copies, sq.at[0], sq_in.at[0])
            z_copies = share_sum(place, sems, sq.at[1], sq_in.at[1], [place.at(dz=i) for i in range(1, 8)])
        spread.steps((parts - 1) * per, parts * per + LAG * 4 + gap * (stages - 1), after)
        if step == 0:
            sq[2] = finish_sum(z_copies, sq.at[1], sq_in.at[1])
            c_copies = share_sum(place, sems, sq.at[2], sq_in.at[2], [place.at(dc=1)])

        def chunk_y(q):
            value = None
            for r in range(parts):
                gram = jnp.concatenate([g_ref[r, i] for i in range(NX)], axis=0)
                term = dot_nn(gram, a_ref[r, q].reshape(wide, a_ref.shape[5]))
                value = term if value is None else value + term
            ykeep[...] = value

        product = [ring_scatter(place, sems, "y", chunk_y, red.at[0], ykeep, *[ybuf.at[step, i] for i in range(6)])]
        pump(product)
        if step == 0:
            sq[3] = finish_sum(c_copies, sq.at[2], sq_in.at[2])
            x_copies = share_sum(place, sems, sq.at[3], sq_in.at[3], [place.at(dx=i) for i in (1, 2, 3)])
        run(*product)
        if step == 0:
            total = jnp.sum(finish_sum(x_copies, sq.at[3], sq_in.at[3]))
            scale2 = jnp.full((8, 128), 1.96 / width, F32) * total
            inv = 1.0 / jnp.sqrt(scale2)
        if step == 0:
            f = jnp.tile(inv[0:1], (1, xo.shape[1] // 128))
            xo[...] = (1.5 * xo[...] - 0.5 * (red[0] * (f * f))) * f
        else:
            xo[...] = math.sqrt(width) * (1.5 * xo[...] - 0.5 * red[0])
        spread.sent()
    s = sems.take()
    mine = pl.ds(pl.multiple_of(place.zh * block, block), block)
    theirs = pl.ds(pl.multiple_of((1 - place.zh) * block, block), block)
    last_out[...] = xo[:, theirs].astype(last_out.dtype)
    swap = sems.copy(last_out, last_in, s, place.at(dz=4))
    swap.start()
    out[place.zh] = xo[:, mine]
    swap.wait()
    out[1 - place.zh] = last_in[...].astype(F32)


def shards(embeddings, rotation, codes, codebooks):
    tok_rows, width = embeddings.shape
    cols = rotation.shape[1]
    subs, centroids, sub_width = codebooks.shape
    rows_total = tok_rows * lax.axis_size("dp")
    block = width // lax.axis_size("dp")
    rebuilt = pl.pallas_call(
        rebuild_kernel,
        out_shape=jax.ShapeDtypeStruct((subs, sub_width, tok_rows), F32),
        in_specs=[pl.BlockSpec(memory_space=pltpu.VMEM)] * 2,
        out_specs=pl.BlockSpec(memory_space=pltpu.VMEM),
        name="rebuild",
    )(codes.T, codebooks.transpose(0, 2, 1)).reshape(cols, tok_rows)
    n = cols // NZH
    m = NZH * block
    panel = m * NY
    parts = PARTS
    rows = n // parts
    wide = NZH * NC * rows
    vm = pltpu.VMEM
    out_t = pl.pallas_call(
        functools.partial(main_kernel, 0.2 * rows_total, width),
        out_shape=jax.ShapeDtypeStruct((NZH, n, block), F32),
        in_specs=[pl.BlockSpec(memory_space=pltpu.VMEM)] * 3,
        out_specs=pl.BlockSpec(memory_space=pltpu.VMEM),
        scratch_shapes=[
            vm((cols, tok_rows), BF), vm((8, tok_rows), F32), vm((NZL * NC - 1, 8, tok_rows), F32),
            vm((n, panel), F32), vm((n, panel), F32),
            vm((2, 6, n, panel), BF), vm((2, 6, n, m), BF),
            vm((n, panel), F32), vm((n, panel), F32),
            vm((2, n, m), F32), vm((n, m), BF), vm((n, m), BF),
            vm((n, m), F32), vm((2, n, m), F32),
            vm((2, NY, n, m), BF), vm((2, parts, NY, NZH, NC, rows, m), BF),
            vm((parts, n, wide), F32), vm((2, parts, 6, n // NX, wide), BF),
            vm((2, parts, NX, n // NX, wide), BF),
            vm((n, m), F32), vm((2, 6, n, m), BF),
            vm((4, 8, 128), F32), vm((4, 7, 8, 128), F32),
            vm((n, block), BF), vm((n, block), BF),
            pltpu.SemaphoreType.DMA((NSEM,)), pltpu.SemaphoreType.DMA((NSEM,)),
        ],
        compiler_params=pltpu.CompilerParams(collective_id=0, has_side_effects=True, vmem_limit_bytes=60 * 2**20),
        name="main",
    )(rebuilt, embeddings, rotation)
    return out_t.reshape(cols, block).T


def solution(mesh):
    placed = (P("dp", None), P(None, "col"), P("dp", "col"), P("col", None, None))
    return jax.shard_map(
        shards, mesh=mesh, in_specs=placed, out_specs=P("dp", "col"), check_vma=False
    )
```

```python
import functools
import math

import jax
import jax.numpy as jnp
from jax import lax
from jax.experimental import pallas as pl
from jax.experimental.pallas import tpu as pltpu
from jax.sharding import PartitionSpec as P

MESH = pl.DeviceIdType.MESH
BF = jnp.bfloat16
F32 = jnp.float32
NX, NY, NZH, NZL, NC = 4, 4, 2, 4, 2
NSEM = 480
LAG = 3
PARTS = 4
PAIR = 2
GAP = 2
SUB = 2


def rebuild_kernel(codes, table, out):
    lanes = 128

    def one_subspace(m, carry):
        entries = table[m].astype(F32)
        ids = codes[pl.ds(m, 1), :]
        for first in range(0, codes.shape[1], lanes):
            index = jnp.broadcast_to(ids[:, first : first + lanes], (entries.shape[0], lanes))
            within = index % lanes
            value = None
            for part in range(entries.shape[1] // lanes):
                picked = jnp.take_along_axis(
                    entries[:, part * lanes : (part + 1) * lanes], within, axis=1, mode="promise_in_bounds"
                )
                value = picked if value is None else jnp.where(index >= part * lanes, picked, value)
            out[m, :, first : first + lanes] = value
        return carry

    lax.fori_loop(0, codes.shape[0], one_subspace, 0, unroll=4)


def dot_nt(a, b):
    return lax.dot_general(a, b, (((1,), (1,)), ((), ())), preferred_element_type=F32)


def dot_nn(a, b):
    return jnp.dot(a, b, preferred_element_type=F32)


class Place:
    def __init__(self):
        dp, col = lax.axis_index("dp"), lax.axis_index("col")
        self.x = dp // (NZH * NY)
        self.zh = (dp // NY) % NZH
        self.y = dp % NY
        self.zl = col // NC
        self.c = col % NC
        self.z = self.zh * NZL + self.zl

    def at(self, dx=0, dy=0, dz=0, dc=0):
        x = (self.x + dx) % NX
        y = (self.y + dy) % NY
        z = (self.z + dz) % (NZH * NZL)
        c = (self.c + dc) % NC
        return (x * (NZH * NY) + (z // NZL) * NY + y, (z % NZL) * NC + c)

    def col_peer(self, i):
        return (lax.axis_index("dp"), (lax.axis_index("col") + i) % (NZL * NC))

    def other_end(self, i):
        zl = (self.zl + i) % NZL
        return (self.x * (NZH * NY) + (1 - self.zh) * NY + self.y, zl * NC + self.c)

    def along(self, axis, step):
        return self.at(dx=step) if axis == "x" else self.at(dy=step)

    def index(self, axis):
        return self.x if axis == "x" else self.y


class Sems:
    def __init__(self, send, recv):
        self.send, self.recv, self.used = send, recv, 0

    def take(self, count=1):
        base = self.used
        self.used += count
        assert self.used <= NSEM
        return base

    def copy(self, src, dst, index, device):
        return pltpu.make_async_remote_copy(
            src_ref=src,
            dst_ref=dst,
            send_sem=self.send.at[index],
            recv_sem=self.recv.at[index],
            device_id=device,
            device_id_type=MESH,
        )


def ring_scatter(place, sems, axis, value, emit, bufs, first, rows, prepare=None):
    diag, got, to_r, to_l, from_l, from_r = bufs
    half = rows // 2
    lo, hi = pl.ds(first, half), pl.ds(first + half, half)
    p = place.index(axis)
    right, left = place.along(axis, 1), place.along(axis, -1)
    s = sems.take(6)
    ready = prepare if prepare is not None else lambda i: None
    ready((p + 2) % 4)
    diag[lo] = value((p + 2) % 4, lo).astype(BF)
    c0 = sems.copy(diag.at[lo], got.at[lo], s, right)
    c0.start()
    diag[hi] = value((p + 2) % 4, hi).astype(BF)
    c1 = sems.copy(diag.at[hi], got.at[hi], s + 1, left)
    c1.start()
    yield
    ready((p + 1) % 4)
    to_r[hi] = value((p + 1) % 4, hi).astype(BF)
    c2 = sems.copy(to_r.at[hi], from_l.at[hi], s + 2, right)
    c2.start()
    ready((p + 3) % 4)
    to_l[lo] = value((p + 3) % 4, lo).astype(BF)
    c4 = sems.copy(to_l.at[lo], from_r.at[lo], s + 4, left)
    c4.start()
    yield
    c0.wait_recv()
    to_r[lo] = (value((p + 1) % 4, lo) + got[lo].astype(F32)).astype(BF)
    c3 = sems.copy(to_r.at[lo], from_l.at[lo], s + 3, right)
    c3.start()
    c1.wait_recv()
    to_l[hi] = (value((p + 3) % 4, hi) + got[hi].astype(F32)).astype(BF)
    c5 = sems.copy(to_l.at[hi], from_r.at[hi], s + 5, left)
    c5.start()
    ready(p)
    yield
    for c in (c2, c3, c4, c5):
        c.wait_recv()
    for part in (lo, hi):
        emit(part, value(p, part) + from_l[part].astype(F32) + from_r[part].astype(F32))
    for c in (c0, c1, c2, c3, c4, c5):
        c.wait_send()


def ring_gather(place, sems, axis, buf, first=0, rows=None):
    rows = buf.shape[1] if rows is None else rows
    half = rows // 2
    all_rows, lo, hi = pl.ds(first, rows), pl.ds(first, half), pl.ds(first + half, half)
    p = place.index(axis)
    right, left = place.along(axis, 1), place.along(axis, -1)
    s = sems.take(4)
    before, after = (p + 3) % 4, (p + 1) % 4
    c0 = sems.copy(buf.at[p, all_rows], buf.at[p, all_rows], s, right)
    c1 = sems.copy(buf.at[p, all_rows], buf.at[p, all_rows], s + 1, left)
    c0.start()
    c1.start()
    yield
    c0.wait_recv()
    c2 = sems.copy(buf.at[before, lo], buf.at[before, lo], s + 2, right)
    c2.start()
    c1.wait_recv()
    c3 = sems.copy(buf.at[after, hi], buf.at[after, hi], s + 3, left)
    c3.start()
    yield
    c2.wait_recv()
    c3.wait_recv()
    for c in (c0, c1, c2, c3):
        c.wait_send()


def run(*gens):
    live = list(gens)
    while live:
        pump(live)


def pump(live):
    for g in list(live):
        if next(g, live) is live:
            live.remove(g)


class Spread:
    def __init__(self, place, sems, bt, at):
        self.place, self.sems, self.bt, self.at = place, sems, bt, at
        z = place.z
        self.d = (place.zl - place.y + 4) % 4
        self.back = (4 - self.d) % 4
        self.up, self.down, self.other = place.at(dz=1), place.at(dz=-1), place.at(dc=1)
        self.up_origin = ((z - self.d + 8) % 8) // 4
        self.down_origin = ((z + self.back) % 8) // 4
        self.parts, self.slots = at.shape[0], at.shape[1] // PAIR
        self.rows = at.shape[4]
        self.count = self.parts * self.slots
        n = self.count
        self.s_up, self.s_down = sems.take(n), sems.take(n)
        self.s_up_half, self.s_down_half = sems.take(n), sems.take(n)
        self.s_core = sems.take(2 * n)

    def spot(self, origin, n, part=None):
        blocks = pl.ds((n % self.slots) * PAIR, PAIR)
        half = self.rows // 2
        rows = pl.ds(0, self.rows) if part is None else pl.ds(part * half, half)
        return self.at.at[n // self.slots, blocks, origin, self.place.c, rows]

    def source(self, n):
        first = pl.multiple_of((n // self.slots) * self.rows, self.rows)
        return self.bt.at[pl.ds((n % self.slots) * PAIR, PAIR), pl.ds(first, self.rows)]

    def full(self, up, n, from_source=False):
        origin = self.up_origin if up else self.down_origin
        src = self.source(n) if from_source else self.spot(origin, n)
        base, device = (self.s_up, self.up) if up else (self.s_down, self.down)
        return self.sems.copy(src, self.spot(origin, n), base + n, device)

    def half(self, up, n, origin):
        part = 0 if up else 1
        base, device = (self.s_up_half, self.up) if up else (self.s_down_half, self.down)
        return self.sems.copy(self.spot(origin, n, part), self.spot(origin, n, part), base + n, device)

    def core(self, origin, n, from_source=False):
        src = self.source(n) if from_source else self.spot(origin, n)
        return self.sems.copy(src, self.spot(origin, n), self.s_core + origin * self.count + n, self.other)

    def steps(self, first, last, after=None):
        d, n_all, far = self.d, self.count, 1 - self.place.zh

        def slot(t, carry):
            @pl.when((d == 0) & (t < n_all))
            def _():
                self.full(True, t, True).start()
                self.full(False, t, True).start()
                self.core(self.place.zh, t, True).start()

            for up, lag, last_d in ((True, d, 3), (False, self.back, 1)):
                origin = self.up_origin if up else self.down_origin
                n = t - LAG * lag

                @pl.when((d > 0) & (n >= 0) & (n < n_all))
                def _(up=up, n=n, last_d=last_d, origin=origin):
                    self.full(up, n).wait_recv()

                    @pl.when(d != last_d)
                    def _():
                        self.full(up, n).start()

                    @pl.when(d == last_d)
                    def _():
                        self.half(up, n, origin).start()

                    self.core(origin, n).start()

            n = t - LAG * 4

            @pl.when((d == 0) & (n >= 0) & (n < n_all))
            def _():
                self.half(True, n, far).wait_recv()
                self.half(False, n, far).wait_recv()
                self.core(far, n).start()

            if after is not None:
                after(t)
            return carry

        lax.fori_loop(first, last, slot, 0)

    def arrived(self, r):
        for q in range(self.slots):
            for origin in range(2):
                self.core(origin, r * self.slots + q).wait_recv()

        @pl.when(self.d == 0)
        def _():
            for q in range(self.slots * PAIR):
                rows = pl.ds(pl.multiple_of(r * self.rows, self.rows), self.rows)
                self.at[r, q, self.place.zh, self.place.c] = self.bt[q, rows]

    def sent(self):
        d = self.d

        def one(n, carry):
            for up, last_d in ((True, 3), (False, 1)):
                origin = self.up_origin if up else self.down_origin

                @pl.when(d != last_d)
                def _(up=up):
                    self.full(up, n).wait_send()

                @pl.when(d == last_d)
                def _(up=up, origin=origin):
                    self.half(up, n, origin).wait_send()

            for origin in range(2):
                self.core(origin, n).wait_send()
            return carry

        lax.fori_loop(0, self.count, one, 0)


class GramReduce:
    def __init__(self, place, sems, spread, keep, bufs, full):
        self.place, self.sems, self.spread = place, sems, spread
        self.keep, self.bufs, self.full = keep, bufs, full
        self.s = sems.take(10 * full.shape[0])
        self.right, self.left = place.at(dx=1), place.at(dx=-1)
        self.rows = full.shape[2]
        self.half = self.rows // 2
        self.lo, self.hi = pl.ds(0, self.half), pl.ds(self.half, self.half)

    def sc(self, r, i):
        diag, got, to_r, to_l, from_l, from_r = [self.bufs.at[r, k] for k in range(6)]
        src, dst, part, device = (
            (diag, got, self.lo, self.right),
            (diag, got, self.hi, self.left),
            (to_r, from_l, self.hi, self.right),
            (to_r, from_l, self.lo, self.right),
            (to_l, from_r, self.lo, self.left),
            (to_l, from_r, self.hi, self.left),
        )[i]
        return self.sems.copy(src.at[part], dst.at[part], self.s + 10 * r + i, device)

    def ga(self, r, i):
        x = self.place.x
        slot, part, device = (
            (x, pl.ds(0, self.rows), self.right),
            (x, pl.ds(0, self.rows), self.left),
            ((x + 3) % 4, self.lo, self.right),
            ((x + 1) % 4, self.hi, self.left),
        )[i]
        ref = self.full.at[r, slot, part]
        return self.sems.copy(ref, ref, self.s + 10 * r + 6 + i, device)

    def mine(self, r, i, part):
        first = i * self.rows + part * self.half
        return self.keep[r, pl.ds(pl.multiple_of(first, self.half), self.half)]

    def stage(self, number, r):
        x = self.place.x
        if number == 0:
            self.spread.arrived(r)
            bt, at = self.spread.bt, self.spread.at
            wide = at.shape[2] * at.shape[3] * at.shape[4]
            total = None
            for q in range(at.shape[1]):
                term = dot_nt(bt[q], at[r, q].reshape(wide, at.shape[5]))
                total = term if total is None else total + term
            self.keep[r] = total
            for part, rows in ((0, self.lo), (1, self.hi)):
                self.bufs[r, 0, rows] = self.mine(r, (x + 2) % 4, part).astype(BF)
            self.sc(r, 0).start()
            self.sc(r, 1).start()
            self.bufs[r, 2, self.hi] = self.mine(r, (x + 1) % 4, 1).astype(BF)
            self.sc(r, 2).start()
            self.bufs[r, 3, self.lo] = self.mine(r, (x + 3) % 4, 0).astype(BF)
            self.sc(r, 4).start()
        elif number == 1:
            self.sc(r, 0).wait_recv()
            got = self.bufs[r, 1, self.lo].astype(F32)
            self.bufs[r, 2, self.lo] = (self.mine(r, (x + 1) % 4, 0) + got).astype(BF)
            self.sc(r, 3).start()
            self.sc(r, 1).wait_recv()
            got = self.bufs[r, 1, self.hi].astype(F32)
            self.bufs[r, 3, self.hi] = (self.mine(r, (x + 3) % 4, 1) + got).astype(BF)
            self.sc(r, 5).start()
        elif number == 2:
            for i in (2, 3, 4, 5):
                self.sc(r, i).wait_recv()
            for part, rows in ((0, self.lo), (1, self.hi)):
                total = self.mine(r, x, part) + self.bufs[r, 4, rows].astype(F32) + self.bufs[r, 5, rows].astype(F32)
                self.full[r, x, rows] = total.astype(BF)
            self.ga(r, 0).start()
            self.ga(r, 1).start()
        elif number == 3:
            self.ga(r, 0).wait_recv()
            self.ga(r, 2).start()
            self.ga(r, 1).wait_recv()
            self.ga(r, 3).start()
        else:
            self.ga(r, 2).wait_recv()
            self.ga(r, 3).wait_recv()
            for i in range(6):
                self.sc(r, i).wait_send()
            for i in range(4):
                self.ga(r, i).wait_send()


def share_sum(place, sems, mine, slots, partners):
    s = sems.take(len(partners))
    copies = [sems.copy(mine, slots.at[i], s + i, device) for i, device in enumerate(partners)]
    for c in copies:
        c.start()
    return copies


def finish_sum(copies, mine, slots):
    for c in copies:
        c.wait()
    total = mine[...]
    for i in range(len(copies)):
        total = total + slots[i]
    return total


def main_kernel(
    prior_scale, width, rebuilt, e, rot, out,
    wt, err, err_in, part_a, part_b, big, small, own_a, own_b, ab, ab_out, ab_in, xo, red,
    bt, at, gkeep, gbuf, gfull, yk, ybuf, sq, sq_in, last_out, last_in,
    send, recv,
):
    place = Place()
    sems = Sems(send, recv)
    barrier = pltpu.get_barrier_semaphore()
    col_peers = [place.col_peer(i) for i in range(1, NZL * NC)]
    partners = (
        [place.at(dx=i) for i in (1, 2, 3)]
        + [place.at(dy=i) for i in (1, 2, 3)]
        + [place.other_end(i) for i in range(NZL)]
        + col_peers
    )
    for device in partners:
        pl.semaphore_signal(barrier, inc=1, device_id=device, device_id_type=MESH)

    tok_rows = e.shape[0]
    step_rows = tok_rows // 2
    for first in range(0, tok_rows, step_rows):
        rotated = dot_nn(e[first : first + step_rows], rot[...])
        residue = rotated.T - rebuilt[:, first : first + step_rows]
        squares = residue * residue
        err[:, first : first + step_rows] = jnp.sum(squares.reshape(squares.shape[0] // 8, 8, step_rows), axis=0)
    pl.semaphore_wait(barrier, len(partners))

    total = jnp.sum(finish_sum(share_sum(place, sems, err, err_in, col_peers), err, err_in), axis=0, keepdims=True)
    weights = 1.0 / (1.0 + total / (2.0 * width))
    wt[...] = (rebuilt[...] * weights).astype(BF)

    block = out.shape[2]
    n_half = wt.shape[0] // 2
    x_cols = e.shape[1] // NX

    def compute_a(xi):
        start = pl.multiple_of(xi * x_cols, x_cols)
        value = dot_nn(wt[0:n_half], e[:, pl.ds(start, x_cols)])
        for zh in range(NZH):
            for y in range(NY):
                at_in, at_out = (zh * NY + y) * block, (y * NZH + zh) * block
                part_a[xi, :, at_out : at_out + block] = value[:, at_in : at_in + block]

    def compute_b(yi):
        parts = []
        for x in range(NX):
            for zh in range(NZH):
                start = pl.multiple_of(x * x_cols + (zh * NY + yi) * block, block)
                parts.append(e[:, pl.ds(start, block)])
        part_b[yi] = dot_nn(wt[n_half:], jnp.concatenate(parts, axis=1))

    sub = n_half // SUB
    m = ab.shape[2]

    def chain(which, k):
        first_axis, second_axis = ("x", "y") if which == 0 else ("y", "x")
        source, own = (part_a, own_a) if which == 0 else (part_b, own_b)
        prepare = (compute_a if which == 0 else compute_b) if k == 0 else None

        def keep_own(rows, total):
            own[rows] = total

        def keep_ab(rows, total):
            ab[which, rows] = total

        yield from ring_scatter(
            place, sems, first_axis, lambda i, rows: source[i, rows], keep_own,
            [big.at[which, i] for i in range(6)], k * sub, sub, prepare,
        )
        yield from ring_scatter(
            place, sems, second_axis, lambda i, rows: own[rows, pl.ds(pl.multiple_of(i * m, m), m)], keep_ab,
            [small.at[which, i] for i in range(6)], k * sub, sub,
        )

    def in_rounds(groups, finished, between=None):
        groups = dict(enumerate(groups))
        count = 0
        while groups:
            if between is not None:
                between(count)
            count += 1
            for k in list(groups):
                pump(groups[k])
                if not groups[k]:
                    del groups[k]
                    finished(k)

    swaps = []

    def start_swap(k):
        rows = pl.ds(k * sub, sub)
        ab_out[rows] = ab[1 - place.zh, rows].astype(BF)
        swap = sems.copy(ab_out.at[rows], ab_in.at[rows], sems.take(), place.at(dz=4))
        swap.start()
        swaps.append(swap)

    for zh in range(NZH):
        rows = pl.ds(pl.multiple_of(place.x * x_cols + (zh * NY + place.y) * block, block), block)
        cols = pl.ds(pl.multiple_of(place.zh * n_half, n_half), n_half)
        xo[:, zh * block : (zh + 1) * block] = prior_scale * rot[rows, cols].astype(F32).T
    in_rounds([[chain(0, k), chain(1, k)] for k in range(SUB)], start_swap)

    parts, rows_r = at.shape[1], at.shape[5]
    wide = NZH * NC * rows_r
    panels = {0: [], 1: []}

    def share_rows(step, k):
        rows = pl.ds(k * sub, sub)
        bt[step, place.y, rows] = xo[rows].astype(BF)
        for r in range(k * parts // SUB, (k + 1) * parts // SUB):
            g = ring_gather(place, sems, "y", bt.at[step], r * rows_r, rows_r)
            next(g)
            panels[step].append(g)

    for k in range(SUB):
        rows = pl.ds(k * sub, sub)
        swaps[k].wait()
        xo[rows] = ab[place.zh, rows] + ab_in[rows].astype(F32) + xo[rows]
        share_rows(0, k)
    squares = xo[...] * xo[...]
    folded = jnp.sum(squares.reshape(squares.shape[0] // 8, 8, squares.shape[1]), axis=0)
    part = folded[:, 0:128]
    for i in range(1, folded.shape[1] // 128):
        part = part + folded[:, i * 128 : (i + 1) * 128]
    sq[0] = part

    y_copies = share_sum(place, sems, sq.at[0], sq_in.at[0], [place.at(dy=i) for i in (1, 2, 3)])
    mine = pl.ds(pl.multiple_of(place.zh * block, block), block)
    theirs = pl.ds(pl.multiple_of((1 - place.zh) * block, block), block)
    last = []
    spreads = []
    for step in range(2):
        b_ref, a_ref, g_ref = bt.at[step], at.at[step], gfull.at[step]
        panel = panels[step]
        spread = Spread(place, sems, b_ref, a_ref)
        spreads.append(spread)
        grams = GramReduce(place, sems, spread, gkeep, gbuf.at[step], g_ref)
        per, gap, stages = spread.slots, spread.slots * GAP, 5
        d = spread.d
        hops = 4 - d + (d // 3) * 2

        def after(t):
            for number in reversed(range(stages)):
                ahead = t - gap * number - (per - 1) - LAG * hops

                @pl.when((ahead >= 0) & (ahead % per == 0) & (ahead < per * parts))
                def _(number=number, ahead=ahead):
                    grams.stage(number, ahead // per)

        run(panel[0])
        for g in panel[1:]:
            next(g)
        for r in range(1, parts):
            spread.steps((r - 1) * per, r * per)
            run(panel[r])
        if step == 0:
            sq[1] = finish_sum(y_copies, sq.at[0], sq_in.at[0])
            z_copies = share_sum(place, sems, sq.at[1], sq_in.at[1], [place.at(dz=i) for i in range(1, 8)])
        spread.steps((parts - 1) * per, parts * per + LAG * 4 + gap * (stages - 1), after)
        if step == 0:
            sq[2] = finish_sum(z_copies, sq.at[1], sq_in.at[1])
            c_copies = share_sum(place, sems, sq.at[2], sq_in.at[2], [place.at(dc=1)])

        def compute_y(q):
            value = None
            for r in range(parts):
                gram = jnp.concatenate([g_ref[r, i] for i in range(NX)], axis=0)
                term = dot_nn(gram, a_ref[r, q].reshape(wide, a_ref.shape[5]))
                value = term if value is None else value + term
            yk[q] = value

        def keep_y(rows, total):
            red[rows] = total

        def sums(count, step=step):
            if step == 0 and count == 1:
                sq[3] = finish_sum(shared["c"], sq.at[2], sq_in.at[2])
                shared["x"] = share_sum(place, sems, sq.at[3], sq_in.at[3], [place.at(dx=i) for i in (1, 2, 3)])
            if step == 0 and count == 3:
                total = jnp.sum(finish_sum(shared["x"], sq.at[3], sq_in.at[3]))
                scale2 = jnp.full((8, 128), 1.96 / width, F32) * total
                shared["inv"] = jnp.tile((1.0 / jnp.sqrt(scale2))[0:1], (1, m // 128))

        def finish_rows(k, step=step):
            rows = pl.ds(k * sub, sub)
            if step == 0:
                f = shared["inv"]
                xo[rows] = (1.5 * xo[rows] - 0.5 * (red[rows] * (f * f))) * f
                share_rows(1, k)
            else:
                xo[rows] = math.sqrt(width) * (1.5 * xo[rows] - 0.5 * red[rows])
                last_out[rows] = xo[rows, theirs].astype(BF)
                swap = sems.copy(last_out.at[rows], last_in.at[rows], sems.take(), place.at(dz=4))
                swap.start()
                last.append(swap)
                out[place.zh, rows] = xo[rows, mine]

        shared = {"c": c_copies if step == 0 else None}
        in_rounds(
            [
                [
                    ring_scatter(
                        place, sems, "y", lambda i, rows: yk[i, rows], keep_y,
                        [ybuf.at[step, i] for i in range(6)], k * sub, sub, compute_y if k == 0 else None,
                    )
                ]
                for k in range(SUB)
            ],
            finish_rows,
            sums,
        )
    for spread in spreads:
        spread.sent()
    for k in range(SUB):
        rows = pl.ds(k * sub, sub)
        last[k].wait()
        out[1 - place.zh, rows] = last_in[rows].astype(F32)


def shards(embeddings, rotation, codes, codebooks):
    tok_rows, width = embeddings.shape
    cols = rotation.shape[1]
    subs, centroids, sub_width = codebooks.shape
    rows_total = tok_rows * lax.axis_size("dp")
    block = width // lax.axis_size("dp")
    rebuilt = pl.pallas_call(
        rebuild_kernel,
        out_shape=jax.ShapeDtypeStruct((subs, sub_width, tok_rows), F32),
        in_specs=[pl.BlockSpec(memory_space=pltpu.VMEM)] * 2,
        out_specs=pl.BlockSpec(memory_space=pltpu.VMEM),
        name="rebuild",
    )(codes.T, codebooks.transpose(0, 2, 1)).reshape(cols, tok_rows)
    n = cols // NZH
    m = NZH * block
    panel = m * NY
    parts = PARTS
    rows = n // parts
    wide = NZH * NC * rows
    vm = pltpu.VMEM
    out_t = pl.pallas_call(
        functools.partial(main_kernel, 0.2 * rows_total, width),
        out_shape=jax.ShapeDtypeStruct((NZH, n, block), F32),
        in_specs=[pl.BlockSpec(memory_space=pltpu.VMEM)] * 3,
        out_specs=pl.BlockSpec(memory_space=pltpu.VMEM),
        scratch_shapes=[
            vm((cols, tok_rows), BF), vm((8, tok_rows), F32), vm((NZL * NC - 1, 8, tok_rows), F32),
            vm((NX, n, panel), F32), vm((NY, n, panel), F32),
            vm((2, 6, n, panel), BF), vm((2, 6, n, m), BF),
            vm((n, panel), F32), vm((n, panel), F32),
            vm((2, n, m), F32), vm((n, m), BF), vm((n, m), BF),
            vm((n, m), F32), vm((n, m), F32),
            vm((2, NY, n, m), BF), vm((2, parts, NY, NZH, NC, rows, m), BF),
            vm((parts, n, wide), F32), vm((2, parts, 6, n // NX, wide), BF),
            vm((2, parts, NX, n // NX, wide), BF),
            vm((NY, n, m), F32), vm((2, 6, n, m), BF),
            vm((4, 8, 128), F32), vm((4, 7, 8, 128), F32),
            vm((n, block), BF), vm((n, block), BF),
            pltpu.SemaphoreType.DMA((NSEM,)), pltpu.SemaphoreType.DMA((NSEM,)),
        ],
        compiler_params=pltpu.CompilerParams(collective_id=0, has_side_effects=True, vmem_limit_bytes=60 * 2**20),
        name="main",
    )(rebuilt, embeddings, rotation)
    return out_t.reshape(cols, block).T


def solution(mesh):
    placed = (P("dp", None), P(None, "col"), P("dp", "col"), P("col", None, None))
    return jax.shard_map(
        shards, mesh=mesh, in_specs=placed, out_specs=P("dp", "col"), check_vma=False
    )
```

```python
import functools
import math

import jax
import jax.numpy as jnp
from jax import lax
from jax.experimental import pallas as pl
from jax.experimental.pallas import tpu as pltpu
from jax.sharding import PartitionSpec as P

MESH = pl.DeviceIdType.MESH
BF = jnp.bfloat16
F32 = jnp.float32
NX, NY, NZH, NZL, NC = 4, 4, 2, 4, 2
NSEM = 560
LAG = 3
PARTS = 4
PAIR = 2
GAP = 3
SUB = 4


def rebuild_kernel(codes, table, out):
    lanes = 128

    def one_subspace(m, carry):
        entries = table[m].astype(F32)
        ids = codes[pl.ds(m, 1), :]
        for first in range(0, codes.shape[1], lanes):
            index = jnp.broadcast_to(ids[:, first : first + lanes], (entries.shape[0], lanes))
            within = index % lanes
            value = None
            for part in range(entries.shape[1] // lanes):
                picked = jnp.take_along_axis(
                    entries[:, part * lanes : (part + 1) * lanes], within, axis=1, mode="promise_in_bounds"
                )
                value = picked if value is None else jnp.where(index >= part * lanes, picked, value)
            out[m, :, first : first + lanes] = value
        return carry

    lax.fori_loop(0, codes.shape[0], one_subspace, 0, unroll=8)


def dot_nt(a, b):
    return lax.dot_general(a, b, (((1,), (1,)), ((), ())), preferred_element_type=F32)


def dot_nn(a, b):
    return jnp.dot(a, b, preferred_element_type=F32)


class Place:
    def __init__(self):
        dp, col = lax.axis_index("dp"), lax.axis_index("col")
        self.x = dp // (NZH * NY)
        self.zh = (dp // NY) % NZH
        self.y = dp % NY
        self.zl = col // NC
        self.c = col % NC
        self.z = self.zh * NZL + self.zl

    def at(self, dx=0, dy=0, dz=0, dc=0):
        x = (self.x + dx) % NX
        y = (self.y + dy) % NY
        z = (self.z + dz) % (NZH * NZL)
        c = (self.c + dc) % NC
        return (x * (NZH * NY) + (z // NZL) * NY + y, (z % NZL) * NC + c)

    def col_peer(self, i):
        return (lax.axis_index("dp"), (lax.axis_index("col") + i) % (NZL * NC))

    def other_end(self, i):
        zl = (self.zl + i) % NZL
        return (self.x * (NZH * NY) + (1 - self.zh) * NY + self.y, zl * NC + self.c)

    def along(self, axis, step):
        return self.at(dx=step) if axis == "x" else self.at(dy=step)

    def index(self, axis):
        return self.x if axis == "x" else self.y


class Sems:
    def __init__(self, send, recv):
        self.send, self.recv, self.used = send, recv, 0

    def take(self, count=1):
        base = self.used
        self.used += count
        assert self.used <= NSEM
        return base

    def copy(self, src, dst, index, device):
        return pltpu.make_async_remote_copy(
            src_ref=src,
            dst_ref=dst,
            send_sem=self.send.at[index],
            recv_sem=self.recv.at[index],
            device_id=device,
            device_id_type=MESH,
        )


def ring_scatter(place, sems, axis, value, emit, bufs, first, rows, prepare=None):
    diag, got, to_r, to_l, from_l, from_r = bufs
    half = rows // 2
    lo, hi = pl.ds(first, half), pl.ds(first + half, half)
    p = place.index(axis)
    right, left = place.along(axis, 1), place.along(axis, -1)
    s = sems.take(6)
    ready = prepare if prepare is not None else lambda i: None
    ready((p + 2) % 4)
    diag[lo] = value((p + 2) % 4, lo).astype(BF)
    c0 = sems.copy(diag.at[lo], got.at[lo], s, right)
    c0.start()
    diag[hi] = value((p + 2) % 4, hi).astype(BF)
    c1 = sems.copy(diag.at[hi], got.at[hi], s + 1, left)
    c1.start()
    yield
    ready((p + 1) % 4)
    to_r[hi] = value((p + 1) % 4, hi).astype(BF)
    c2 = sems.copy(to_r.at[hi], from_l.at[hi], s + 2, right)
    c2.start()
    ready((p + 3) % 4)
    to_l[lo] = value((p + 3) % 4, lo).astype(BF)
    c4 = sems.copy(to_l.at[lo], from_r.at[lo], s + 4, left)
    c4.start()
    yield
    c0.wait_recv()
    to_r[lo] = (value((p + 1) % 4, lo) + got[lo].astype(F32)).astype(BF)
    c3 = sems.copy(to_r.at[lo], from_l.at[lo], s + 3, right)
    c3.start()
    c1.wait_recv()
    to_l[hi] = (value((p + 3) % 4, hi) + got[hi].astype(F32)).astype(BF)
    c5 = sems.copy(to_l.at[hi], from_r.at[hi], s + 5, left)
    c5.start()
    ready(p)
    yield
    for c in (c2, c3, c4, c5):
        c.wait_recv()
    for part in (lo, hi):
        emit(part, value(p, part) + from_l[part].astype(F32) + from_r[part].astype(F32))
    for c in (c0, c1, c2, c3, c4, c5):
        c.wait_send()


def ring_gather(place, sems, axis, buf, first=0, rows=None):
    rows = buf.shape[1] if rows is None else rows
    half = rows // 2
    all_rows, lo, hi = pl.ds(first, rows), pl.ds(first, half), pl.ds(first + half, half)
    p = place.index(axis)
    right, left = place.along(axis, 1), place.along(axis, -1)
    s = sems.take(4)
    before, after = (p + 3) % 4, (p + 1) % 4
    c0 = sems.copy(buf.at[p, all_rows], buf.at[p, all_rows], s, right)
    c1 = sems.copy(buf.at[p, all_rows], buf.at[p, all_rows], s + 1, left)
    c0.start()
    c1.start()
    yield
    c0.wait_recv()
    c2 = sems.copy(buf.at[before, lo], buf.at[before, lo], s + 2, right)
    c2.start()
    c1.wait_recv()
    c3 = sems.copy(buf.at[after, hi], buf.at[after, hi], s + 3, left)
    c3.start()
    yield
    c2.wait_recv()
    c3.wait_recv()
    for c in (c0, c1, c2, c3):
        c.wait_send()


def run(*gens):
    live = list(gens)
    while live:
        pump(live)


def pump(live):
    for g in list(live):
        if next(g, live) is live:
            live.remove(g)


class Spread:
    def __init__(self, place, sems, bt, at):
        self.place, self.sems, self.bt, self.at = place, sems, bt, at
        z = place.z
        self.d = (place.zl - place.y + 4) % 4
        self.back = (4 - self.d) % 4
        self.up, self.down, self.other = place.at(dz=1), place.at(dz=-1), place.at(dc=1)
        self.up_origin = ((z - self.d + 8) % 8) // 4
        self.down_origin = ((z + self.back) % 8) // 4
        self.parts, self.slots = at.shape[0], at.shape[1] // PAIR
        self.rows = at.shape[4]
        self.count = self.parts * self.slots
        n = self.count
        self.s_up, self.s_down = sems.take(n), sems.take(n)
        self.s_up_half, self.s_down_half = sems.take(n), sems.take(n)
        self.s_core = sems.take(2 * n)

    def spot(self, origin, n, part=None):
        blocks = pl.ds((n % self.slots) * PAIR, PAIR)
        half = self.rows // 2
        rows = pl.ds(0, self.rows) if part is None else pl.ds(part * half, half)
        return self.at.at[n // self.slots, blocks, origin, self.place.c, rows]

    def source(self, n):
        first = pl.multiple_of((n // self.slots) * self.rows, self.rows)
        return self.bt.at[pl.ds((n % self.slots) * PAIR, PAIR), pl.ds(first, self.rows)]

    def full(self, up, n, from_source=False):
        origin = self.up_origin if up else self.down_origin
        src = self.source(n) if from_source else self.spot(origin, n)
        base, device = (self.s_up, self.up) if up else (self.s_down, self.down)
        return self.sems.copy(src, self.spot(origin, n), base + n, device)

    def half(self, up, n, origin):
        part = 0 if up else 1
        base, device = (self.s_up_half, self.up) if up else (self.s_down_half, self.down)
        return self.sems.copy(self.spot(origin, n, part), self.spot(origin, n, part), base + n, device)

    def core(self, origin, n, from_source=False):
        src = self.source(n) if from_source else self.spot(origin, n)
        return self.sems.copy(src, self.spot(origin, n), self.s_core + origin * self.count + n, self.other)

    def steps(self, first, last, after=None):
        d, n_all, far = self.d, self.count, 1 - self.place.zh

        def slot(t, carry):
            @pl.when((d == 0) & (t < n_all))
            def _():
                self.full(True, t, True).start()
                self.full(False, t, True).start()
                self.core(self.place.zh, t, True).start()

            for up, lag, last_d in ((True, d, 3), (False, self.back, 1)):
                origin = self.up_origin if up else self.down_origin
                n = t - LAG * lag

                @pl.when((d > 0) & (n >= 0) & (n < n_all))
                def _(up=up, n=n, last_d=last_d, origin=origin):
                    self.full(up, n).wait_recv()

                    @pl.when(d != last_d)
                    def _():
                        self.full(up, n).start()

                    @pl.when(d == last_d)
                    def _():
                        self.half(up, n, origin).start()

                    self.core(origin, n).start()

            n = t - LAG * 4

            @pl.when((d == 0) & (n >= 0) & (n < n_all))
            def _():
                self.half(True, n, far).wait_recv()
                self.half(False, n, far).wait_recv()
                self.core(far, n).start()

            if after is not None:
                after(t)
            return carry

        lax.fori_loop(first, last, slot, 0)

    def arrived(self, r):
        for q in range(self.slots):
            for origin in range(2):
                self.core(origin, r * self.slots + q).wait_recv()

        @pl.when(self.d == 0)
        def _():
            for q in range(self.slots * PAIR):
                rows = pl.ds(pl.multiple_of(r * self.rows, self.rows), self.rows)
                self.at[r, q, self.place.zh, self.place.c] = self.bt[q, rows]

    def sent(self):
        d = self.d

        def one(n, carry):
            for up, last_d in ((True, 3), (False, 1)):
                origin = self.up_origin if up else self.down_origin

                @pl.when(d != last_d)
                def _(up=up):
                    self.full(up, n).wait_send()

                @pl.when(d == last_d)
                def _(up=up, origin=origin):
                    self.half(up, n, origin).wait_send()

            for origin in range(2):
                self.core(origin, n).wait_send()
            return carry

        lax.fori_loop(0, self.count, one, 0)


class GramReduce:
    def __init__(self, place, sems, spread, keep, bufs, full):
        self.place, self.sems, self.spread = place, sems, spread
        self.keep, self.bufs, self.full = keep, bufs, full
        self.s = sems.take(10 * full.shape[0])
        self.right, self.left = place.at(dx=1), place.at(dx=-1)
        self.rows = full.shape[2]
        self.half = self.rows // 2
        self.lo, self.hi = pl.ds(0, self.half), pl.ds(self.half, self.half)

    def sc(self, r, i):
        diag, got, to_r, to_l, from_l, from_r = [self.bufs.at[r, k] for k in range(6)]
        src, dst, part, device = (
            (diag, got, self.lo, self.right),
            (diag, got, self.hi, self.left),
            (to_r, from_l, self.hi, self.right),
            (to_r, from_l, self.lo, self.right),
            (to_l, from_r, self.lo, self.left),
            (to_l, from_r, self.hi, self.left),
        )[i]
        return self.sems.copy(src.at[part], dst.at[part], self.s + 10 * r + i, device)

    def ga(self, r, i):
        x = self.place.x
        slot, part, device = (
            (x, pl.ds(0, self.rows), self.right),
            (x, pl.ds(0, self.rows), self.left),
            ((x + 3) % 4, self.lo, self.right),
            ((x + 1) % 4, self.hi, self.left),
        )[i]
        ref = self.full.at[r, slot, part]
        return self.sems.copy(ref, ref, self.s + 10 * r + 6 + i, device)

    def mine(self, r, i, part):
        first = i * self.rows + part * self.half
        return self.keep[r, pl.ds(pl.multiple_of(first, self.half), self.half)]

    def stage(self, number, r):
        x = self.place.x
        if number == 0:
            self.spread.arrived(r)
            bt, at = self.spread.bt, self.spread.at
            wide = at.shape[2] * at.shape[3] * at.shape[4]
            total = None
            for q in range(at.shape[1]):
                term = dot_nt(bt[q], at[r, q].reshape(wide, at.shape[5]))
                total = term if total is None else total + term
            self.keep[r] = total
            for part, rows in ((0, self.lo), (1, self.hi)):
                self.bufs[r, 0, rows] = self.mine(r, (x + 2) % 4, part).astype(BF)
            self.sc(r, 0).start()
            self.sc(r, 1).start()
            self.bufs[r, 2, self.hi] = self.mine(r, (x + 1) % 4, 1).astype(BF)
            self.sc(r, 2).start()
            self.bufs[r, 3, self.lo] = self.mine(r, (x + 3) % 4, 0).astype(BF)
            self.sc(r, 4).start()
        elif number == 1:
            self.sc(r, 0).wait_recv()
            got = self.bufs[r, 1, self.lo].astype(F32)
            self.bufs[r, 2, self.lo] = (self.mine(r, (x + 1) % 4, 0) + got).astype(BF)
            self.sc(r, 3).start()
            self.sc(r, 1).wait_recv()
            got = self.bufs[r, 1, self.hi].astype(F32)
            self.bufs[r, 3, self.hi] = (self.mine(r, (x + 3) % 4, 1) + got).astype(BF)
            self.sc(r, 5).start()
        elif number == 2:
            for i in (2, 3, 4, 5):
                self.sc(r, i).wait_recv()
            for part, rows in ((0, self.lo), (1, self.hi)):
                total = self.mine(r, x, part) + self.bufs[r, 4, rows].astype(F32) + self.bufs[r, 5, rows].astype(F32)
                self.full[r, x, rows] = total.astype(BF)
            self.ga(r, 0).start()
            self.ga(r, 1).start()
        elif number == 3:
            self.ga(r, 0).wait_recv()
            self.ga(r, 2).start()
            self.ga(r, 1).wait_recv()
            self.ga(r, 3).start()
        else:
            self.ga(r, 2).wait_recv()
            self.ga(r, 3).wait_recv()
            for i in range(6):
                self.sc(r, i).wait_send()
            for i in range(4):
                self.ga(r, i).wait_send()


def share_sum(place, sems, mine, slots, partners):
    s = sems.take(len(partners))
    copies = [sems.copy(mine, slots.at[i], s + i, device) for i, device in enumerate(partners)]
    for c in copies:
        c.start()
    return copies


def finish_sum(copies, mine, slots):
    for c in copies:
        c.wait()
    total = mine[...]
    for i in range(len(copies)):
        total = total + slots[i]
    return total


def main_kernel(
    prior_scale, width, rebuilt, e_far, rot_far, out,
    e, rot, near, wt, err, err_in, part_a, part_b, big, small, own_a, own_b, ab, ab_out, ab_in, xo, red,
    bt, at, gkeep, gbuf, gfull, yk, ybuf, sq, sq_in, last_out, last_in,
    send, recv,
):
    tok_rows = e.shape[0]
    step_rows = tok_rows // 2
    staged = [pltpu.make_async_copy(rot_far, rot, near.at[0])]
    for i in range(2):
        rows = pl.ds(i * step_rows, step_rows)
        staged.append(pltpu.make_async_copy(e_far.at[rows], e.at[rows], near.at[1 + i]))
    for copy in staged:
        copy.start()
    place = Place()
    sems = Sems(send, recv)
    barrier = pltpu.get_barrier_semaphore()
    col_peers = [place.col_peer(i) for i in range(1, NZL * NC)]
    partners = (
        [place.at(dx=i) for i in (1, 2, 3)]
        + [place.at(dy=i) for i in (1, 2, 3)]
        + [place.other_end(i) for i in range(NZL)]
        + col_peers
    )
    for device in partners:
        pl.semaphore_signal(barrier, inc=1, device_id=device, device_id_type=MESH)

    staged[0].wait()
    for first in range(0, tok_rows, step_rows):
        staged[1 + first // step_rows].wait()
        rotated = dot_nn(e[first : first + step_rows], rot[...])
        residue = rotated.T - rebuilt[:, first : first + step_rows]
        squares = residue * residue
        err[:, first : first + step_rows] = jnp.sum(squares.reshape(squares.shape[0] // 8, 8, step_rows), axis=0)
    pl.semaphore_wait(barrier, len(partners))

    total = jnp.sum(finish_sum(share_sum(place, sems, err, err_in, col_peers), err, err_in), axis=0, keepdims=True)
    weights = 1.0 / (1.0 + total / (2.0 * width))
    wt[...] = (rebuilt[...] * weights).astype(BF)

    block = out.shape[2]
    n_half = wt.shape[0] // 2
    x_cols = e.shape[1] // NX

    def compute_a(xi):
        start = pl.multiple_of(xi * x_cols, x_cols)
        value = dot_nn(wt[0:n_half], e[:, pl.ds(start, x_cols)])
        for zh in range(NZH):
            for y in range(NY):
                at_in, at_out = (zh * NY + y) * block, (y * NZH + zh) * block
                part_a[xi, :, at_out : at_out + block] = value[:, at_in : at_in + block]

    def compute_b(yi):
        parts = []
        for x in range(NX):
            for zh in range(NZH):
                start = pl.multiple_of(x * x_cols + (zh * NY + yi) * block, block)
                parts.append(e[:, pl.ds(start, block)])
        part_b[yi] = dot_nn(wt[n_half:], jnp.concatenate(parts, axis=1))

    sub = n_half // SUB
    m = ab.shape[2]

    def chain(which, k):
        first_axis, second_axis = ("x", "y") if which == 0 else ("y", "x")
        source, own = (part_a, own_a) if which == 0 else (part_b, own_b)
        prepare = (compute_a if which == 0 else compute_b) if k == 0 else None

        def keep_own(rows, total):
            own[rows] = total

        def keep_ab(rows, total):
            ab[which, rows] = total

        yield from ring_scatter(
            place, sems, first_axis, lambda i, rows: source[i, rows], keep_own,
            [big.at[which, i] for i in range(6)], k * sub, sub, prepare,
        )
        yield from ring_scatter(
            place, sems, second_axis, lambda i, rows: own[rows, pl.ds(pl.multiple_of(i * m, m), m)], keep_ab,
            [small.at[which, i] for i in range(6)], k * sub, sub,
        )

    def in_rounds(groups, finished, between=None):
        groups = dict(enumerate(groups))
        count = 0
        while groups:
            if between is not None:
                between(count)
            count += 1
            for k in list(groups):
                pump(groups[k])
                if not groups[k]:
                    del groups[k]
                    finished(k)

    swaps = []

    def start_swap(k):
        rows = pl.ds(k * sub, sub)
        ab_out[rows] = ab[1 - place.zh, rows].astype(BF)
        swap = sems.copy(ab_out.at[rows], ab_in.at[rows], sems.take(), place.at(dz=4))
        swap.start()
        swaps.append(swap)

    for zh in range(NZH):
        rows = pl.ds(pl.multiple_of(place.x * x_cols + (zh * NY + place.y) * block, block), block)
        cols = pl.ds(pl.multiple_of(place.zh * n_half, n_half), n_half)
        xo[:, zh * block : (zh + 1) * block] = prior_scale * rot[rows, cols].astype(F32).T
    in_rounds([[chain(0, k), chain(1, k)] for k in range(SUB)], start_swap)

    parts, rows_r = at.shape[1], at.shape[5]
    wide = NZH * NC * rows_r
    panels = {0: [], 1: []}

    def share_rows(step, k):
        rows = pl.ds(k * sub, sub)
        bt[step, place.y, rows] = xo[rows].astype(BF)
        for r in range(k * parts // SUB, (k + 1) * parts // SUB):
            g = ring_gather(place, sems, "y", bt.at[step], r * rows_r, rows_r)
            next(g)
            panels[step].append(g)

    for k in range(SUB):
        rows = pl.ds(k * sub, sub)
        swaps[k].wait()
        xo[rows] = ab[place.zh, rows] + ab_in[rows].astype(F32) + xo[rows]
        share_rows(0, k)
    squares = xo[...] * xo[...]
    folded = jnp.sum(squares.reshape(squares.shape[0] // 8, 8, squares.shape[1]), axis=0)
    part = folded[:, 0:128]
    for i in range(1, folded.shape[1] // 128):
        part = part + folded[:, i * 128 : (i + 1) * 128]
    sq[0] = part

    y_copies = share_sum(place, sems, sq.at[0], sq_in.at[0], [place.at(dy=i) for i in (1, 2, 3)])
    mine = pl.ds(pl.multiple_of(place.zh * block, block), block)
    theirs = pl.ds(pl.multiple_of((1 - place.zh) * block, block), block)
    last = []
    spreads = []
    for step in range(2):
        b_ref, a_ref, g_ref = bt.at[step], at.at[step], gfull.at[step]
        panel = panels[step]
        spread = Spread(place, sems, b_ref, a_ref)
        spreads.append(spread)
        grams = GramReduce(place, sems, spread, gkeep, gbuf.at[step], g_ref)
        per, gap, stages = spread.slots, spread.slots * GAP, 5
        d = spread.d
        hops = 4 - d + (d // 3) * 2

        def after(t):
            for number in reversed(range(stages)):
                ahead = t - gap * number - (per - 1) - LAG * hops

                @pl.when((ahead >= 0) & (ahead % per == 0) & (ahead < per * parts))
                def _(number=number, ahead=ahead):
                    grams.stage(number, ahead // per)

        run(panel[0])
        for g in panel[1:]:
            next(g)
        for r in range(1, parts):
            spread.steps((r - 1) * per, r * per)
            run(panel[r])
        if step == 0:
            sq[1] = finish_sum(y_copies, sq.at[0], sq_in.at[0])
            z_copies = share_sum(place, sems, sq.at[1], sq_in.at[1], [place.at(dz=i) for i in range(1, 8)])
        spread.steps((parts - 1) * per, parts * per + LAG * 4 + gap * (stages - 1), after)
        if step == 0:
            sq[2] = finish_sum(z_copies, sq.at[1], sq_in.at[1])
            c_copies = share_sum(place, sems, sq.at[2], sq_in.at[2], [place.at(dc=1)])

        def compute_y(q):
            value = None
            for r in range(parts):
                gram = jnp.concatenate([g_ref[r, i] for i in range(NX)], axis=0)
                term = dot_nn(gram, a_ref[r, q].reshape(wide, a_ref.shape[5]))
                value = term if value is None else value + term
            yk[q] = value

        def keep_y(rows, total):
            red[rows] = total

        def sums(count, step=step):
            if step == 0 and count == 1:
                sq[3] = finish_sum(shared["c"], sq.at[2], sq_in.at[2])
                shared["x"] = share_sum(place, sems, sq.at[3], sq_in.at[3], [place.at(dx=i) for i in (1, 2, 3)])
            if step == 0 and count == 3:
                total = jnp.sum(finish_sum(shared["x"], sq.at[3], sq_in.at[3]))
                scale2 = jnp.full((8, 128), 1.96 / width, F32) * total
                shared["inv"] = jnp.tile((1.0 / jnp.sqrt(scale2))[0:1], (1, m // 128))

        def finish_rows(k, step=step):
            rows = pl.ds(k * sub, sub)
            if step == 0:
                f = shared["inv"]
                xo[rows] = (1.5 * xo[rows] - 0.5 * (red[rows] * (f * f))) * f
                share_rows(1, k)
            else:
                xo[rows] = math.sqrt(width) * (1.5 * xo[rows] - 0.5 * red[rows])
                last_out[rows] = xo[rows, theirs].astype(BF)
                swap = sems.copy(last_out.at[rows], last_in.at[rows], sems.take(), place.at(dz=4))
                swap.start()
                last.append(swap)
                out[place.zh, rows] = xo[rows, mine]

        shared = {"c": c_copies if step == 0 else None}
        in_rounds(
            [
                [
                    ring_scatter(
                        place, sems, "y", lambda i, rows: yk[i, rows], keep_y,
                        [ybuf.at[step, i] for i in range(6)], k * sub, sub, compute_y if k == 0 else None,
                    )
                ]
                for k in range(SUB)
            ],
            finish_rows,
            sums,
        )
    for spread in spreads:
        spread.sent()
    for k in range(SUB):
        rows = pl.ds(k * sub, sub)
        last[k].wait()
        out[1 - place.zh, rows] = last_in[rows].astype(F32)


def shards(embeddings, rotation, codes, codebooks):
    tok_rows, width = embeddings.shape
    cols = rotation.shape[1]
    subs, centroids, sub_width = codebooks.shape
    rows_total = tok_rows * lax.axis_size("dp")
    block = width // lax.axis_size("dp")
    rebuilt = pl.pallas_call(
        rebuild_kernel,
        out_shape=jax.ShapeDtypeStruct((subs, sub_width, tok_rows), F32),
        in_specs=[pl.BlockSpec(memory_space=pltpu.VMEM)] * 2,
        out_specs=pl.BlockSpec(memory_space=pltpu.VMEM),
        name="rebuild",
    )(codes.T, codebooks.transpose(0, 2, 1)).reshape(cols, tok_rows)
    n = cols // NZH
    m = NZH * block
    panel = m * NY
    parts = PARTS
    rows = n // parts
    wide = NZH * NC * rows
    vm = pltpu.VMEM
    out_t = pl.pallas_call(
        functools.partial(main_kernel, 0.2 * rows_total, width),
        out_shape=jax.ShapeDtypeStruct((NZH, n, block), F32),
        in_specs=[pl.BlockSpec(memory_space=pltpu.VMEM)] + [pl.BlockSpec(memory_space=pl.ANY)] * 2,
        out_specs=pl.BlockSpec(memory_space=pltpu.VMEM),
        scratch_shapes=[
            vm((tok_rows, width), BF), vm((width, cols), BF), pltpu.SemaphoreType.DMA((3,)),
            vm((cols, tok_rows), BF), vm((8, tok_rows), F32), vm((NZL * NC - 1, 8, tok_rows), F32),
            vm((NX, n, panel), F32), vm((NY, n, panel), F32),
            vm((2, 6, n, panel), BF), vm((2, 6, n, m), BF),
            vm((n, panel), F32), vm((n, panel), F32),
            vm((2, n, m), F32), vm((n, m), BF), vm((n, m), BF),
            vm((n, m), F32), vm((n, m), F32),
            vm((2, NY, n, m), BF), vm((2, parts, NY, NZH, NC, rows, m), BF),
            vm((parts, n, wide), F32), vm((2, parts, 6, n // NX, wide), BF),
            vm((2, parts, NX, n // NX, wide), BF),
            vm((NY, n, m), F32), vm((2, 6, n, m), BF),
            vm((4, 8, 128), F32), vm((4, 7, 8, 128), F32),
            vm((n, block), BF), vm((n, block), BF),
            pltpu.SemaphoreType.DMA((NSEM,)), pltpu.SemaphoreType.DMA((NSEM,)),
        ],
        compiler_params=pltpu.CompilerParams(collective_id=0, has_side_effects=True, vmem_limit_bytes=60 * 2**20),
        name="main",
    )(rebuilt, embeddings, rotation)
    return out_t.reshape(cols, block).T


def solution(mesh):
    placed = (P("dp", None), P(None, "col"), P("dp", "col"), P("col", None, None))
    return jax.shard_map(
        shards, mesh=mesh, in_specs=placed, out_specs=P("dp", "col"), check_vma=False
    )
```

```python
import functools
import math

import jax
import jax.numpy as jnp
from jax import lax
from jax.experimental import pallas as pl
from jax.experimental.pallas import tpu as pltpu
from jax.sharding import PartitionSpec as P

MESH = pl.DeviceIdType.MESH
BF = jnp.bfloat16
F32 = jnp.float32
NX, NY, NZH, NZL, NC = 4, 4, 2, 4, 2
NSEM = 560
LAG = 3
PARTS = 4
PAIR = 2
GAP = 3
SUB = 4


def rebuild_kernel(codes, table, out):
    lanes = 128

    def one_subspace(m, carry):
        entries = table[m].astype(F32)
        ids = codes[pl.ds(m, 1), :]
        for first in range(0, codes.shape[1], lanes):
            index = jnp.broadcast_to(ids[:, first : first + lanes], (entries.shape[0], lanes))
            within = index & (lanes - 1)
            value = None
            for part in range(entries.shape[1] // lanes):
                picked = jnp.take_along_axis(
                    entries[:, part * lanes : (part + 1) * lanes], within, axis=1, mode="promise_in_bounds"
                )
                value = picked if value is None else jnp.where(index >= part * lanes, picked, value)
            out[m, :, first : first + lanes] = value
        return carry

    lax.fori_loop(0, codes.shape[0], one_subspace, 0, unroll=8)


def dot_nt(a, b):
    return lax.dot_general(a, b, (((1,), (1,)), ((), ())), preferred_element_type=F32)


def dot_nn(a, b):
    return jnp.dot(a, b, preferred_element_type=F32)


class Place:
    def __init__(self):
        dp, col = lax.axis_index("dp"), lax.axis_index("col")
        self.x = dp // (NZH * NY)
        self.zh = (dp // NY) % NZH
        self.y = dp % NY
        self.zl = col // NC
        self.c = col % NC
        self.z = self.zh * NZL + self.zl

    def at(self, dx=0, dy=0, dz=0, dc=0):
        x = (self.x + dx) % NX
        y = (self.y + dy) % NY
        z = (self.z + dz) % (NZH * NZL)
        c = (self.c + dc) % NC
        return (x * (NZH * NY) + (z // NZL) * NY + y, (z % NZL) * NC + c)

    def col_peer(self, i):
        return (lax.axis_index("dp"), (lax.axis_index("col") + i) % (NZL * NC))

    def other_end(self, i):
        zl = (self.zl + i) % NZL
        return (self.x * (NZH * NY) + (1 - self.zh) * NY + self.y, zl * NC + self.c)

    def along(self, axis, step):
        return self.at(dx=step) if axis == "x" else self.at(dy=step)

    def index(self, axis):
        return self.x if axis == "x" else self.y


class Sems:
    def __init__(self, send, recv):
        self.send, self.recv, self.used = send, recv, 0

    def take(self, count=1):
        base = self.used
        self.used += count
        assert self.used <= NSEM
        return base

    def copy(self, src, dst, index, device):
        return pltpu.make_async_remote_copy(
            src_ref=src,
            dst_ref=dst,
            send_sem=self.send.at[index],
            recv_sem=self.recv.at[index],
            device_id=device,
            device_id_type=MESH,
        )


def ring_scatter(place, sems, axis, value, emit, bufs, first, rows, prepare=None):
    diag, got, to_r, to_l, from_l, from_r = bufs
    half = rows // 2
    lo, hi = pl.ds(first, half), pl.ds(first + half, half)
    p = place.index(axis)
    right, left = place.along(axis, 1), place.along(axis, -1)
    s = sems.take(6)
    ready = prepare if prepare is not None else lambda i: None
    ready((p + 2) % 4)
    diag[lo] = value((p + 2) % 4, lo).astype(BF)
    c0 = sems.copy(diag.at[lo], got.at[lo], s, right)
    c0.start()
    diag[hi] = value((p + 2) % 4, hi).astype(BF)
    c1 = sems.copy(diag.at[hi], got.at[hi], s + 1, left)
    c1.start()
    yield
    ready((p + 1) % 4)
    to_r[hi] = value((p + 1) % 4, hi).astype(BF)
    c2 = sems.copy(to_r.at[hi], from_l.at[hi], s + 2, right)
    c2.start()
    ready((p + 3) % 4)
    to_l[lo] = value((p + 3) % 4, lo).astype(BF)
    c4 = sems.copy(to_l.at[lo], from_r.at[lo], s + 4, left)
    c4.start()
    yield
    c0.wait_recv()
    to_r[lo] = (value((p + 1) % 4, lo) + got[lo].astype(F32)).astype(BF)
    c3 = sems.copy(to_r.at[lo], from_l.at[lo], s + 3, right)
    c3.start()
    c1.wait_recv()
    to_l[hi] = (value((p + 3) % 4, hi) + got[hi].astype(F32)).astype(BF)
    c5 = sems.copy(to_l.at[hi], from_r.at[hi], s + 5, left)
    c5.start()
    ready(p)
    yield
    for c in (c2, c3, c4, c5):
        c.wait_recv()
    for part in (lo, hi):
        emit(part, value(p, part) + from_l[part].astype(F32) + from_r[part].astype(F32))
    for c in (c0, c1, c2, c3, c4, c5):
        c.wait_send()


def ring_gather(place, sems, axis, buf, first=0, rows=None):
    rows = buf.shape[1] if rows is None else rows
    half = rows // 2
    all_rows, lo, hi = pl.ds(first, rows), pl.ds(first, half), pl.ds(first + half, half)
    p = place.index(axis)
    right, left = place.along(axis, 1), place.along(axis, -1)
    s = sems.take(4)
    before, after = (p + 3) % 4, (p + 1) % 4
    c0 = sems.copy(buf.at[p, all_rows], buf.at[p, all_rows], s, right)
    c1 = sems.copy(buf.at[p, all_rows], buf.at[p, all_rows], s + 1, left)
    c0.start()
    c1.start()
    yield
    c0.wait_recv()
    c2 = sems.copy(buf.at[before, lo], buf.at[before, lo], s + 2, right)
    c2.start()
    c1.wait_recv()
    c3 = sems.copy(buf.at[after, hi], buf.at[after, hi], s + 3, left)
    c3.start()
    yield
    c2.wait_recv()
    c3.wait_recv()
    for c in (c0, c1, c2, c3):
        c.wait_send()


def run(*gens):
    live = list(gens)
    while live:
        pump(live)


def pump(live):
    for g in list(live):
        if next(g, live) is live:
            live.remove(g)


class Spread:
    def __init__(self, place, sems, bt, at):
        self.place, self.sems, self.bt, self.at = place, sems, bt, at
        z = place.z
        self.d = (place.zl - place.y + 4) % 4
        self.back = (4 - self.d) % 4
        self.up, self.down, self.other = place.at(dz=1), place.at(dz=-1), place.at(dc=1)
        self.up_origin = ((z - self.d + 8) % 8) // 4
        self.down_origin = ((z + self.back) % 8) // 4
        self.parts, self.slots = at.shape[0], at.shape[1] // PAIR
        self.rows = at.shape[4]
        self.count = self.parts * self.slots
        n = self.count
        self.s_up, self.s_down = sems.take(n), sems.take(n)
        self.s_up_half, self.s_down_half = sems.take(n), sems.take(n)
        self.s_core = sems.take(2 * n)

    def spot(self, origin, n, part=None):
        blocks = pl.ds((n % self.slots) * PAIR, PAIR)
        half = self.rows // 2
        rows = pl.ds(0, self.rows) if part is None else pl.ds(part * half, half)
        return self.at.at[n // self.slots, blocks, origin, self.place.c, rows]

    def source(self, n):
        first = pl.multiple_of((n // self.slots) * self.rows, self.rows)
        return self.bt.at[pl.ds((n % self.slots) * PAIR, PAIR), pl.ds(first, self.rows)]

    def full(self, up, n, from_source=False):
        origin = self.up_origin if up else self.down_origin
        src = self.source(n) if from_source else self.spot(origin, n)
        base, device = (self.s_up, self.up) if up else (self.s_down, self.down)
        return self.sems.copy(src, self.spot(origin, n), base + n, device)

    def half(self, up, n, origin):
        part = 0 if up else 1
        base, device = (self.s_up_half, self.up) if up else (self.s_down_half, self.down)
        return self.sems.copy(self.spot(origin, n, part), self.spot(origin, n, part), base + n, device)

    def core(self, origin, n, from_source=False):
        src = self.source(n) if from_source else self.spot(origin, n)
        return self.sems.copy(src, self.spot(origin, n), self.s_core + origin * self.count + n, self.other)

    def steps(self, first, last, after=None):
        d, n_all, far = self.d, self.count, 1 - self.place.zh

        def slot(t, carry):
            @pl.when((d == 0) & (t < n_all))
            def _():
                self.full(True, t, True).start()
                self.full(False, t, True).start()
                self.core(self.place.zh, t, True).start()

            for up, lag, last_d in ((True, d, 3), (False, self.back, 1)):
                origin = self.up_origin if up else self.down_origin
                n = t - LAG * lag

                @pl.when((d > 0) & (n >= 0) & (n < n_all))
                def _(up=up, n=n, last_d=last_d, origin=origin):
                    self.full(up, n).wait_recv()

                    @pl.when(d != last_d)
                    def _():
                        self.full(up, n).start()

                    @pl.when(d == last_d)
                    def _():
                        self.half(up, n, origin).start()

                    self.core(origin, n).start()

            n = t - LAG * 4

            @pl.when((d == 0) & (n >= 0) & (n < n_all))
            def _():
                self.half(True, n, far).wait_recv()
                self.half(False, n, far).wait_recv()
                self.core(far, n).start()

            if after is not None:
                after(t)
            return carry

        lax.fori_loop(first, last, slot, 0)

    def arrived(self, r):
        for q in range(self.slots):
            for origin in range(2):
                self.core(origin, r * self.slots + q).wait_recv()

        @pl.when(self.d == 0)
        def _():
            for q in range(self.slots * PAIR):
                rows = pl.ds(pl.multiple_of(r * self.rows, self.rows), self.rows)
                self.at[r, q, self.place.zh, self.place.c] = self.bt[q, rows]

    def sent(self):
        d = self.d

        def one(n, carry):
            for up, last_d in ((True, 3), (False, 1)):
                origin = self.up_origin if up else self.down_origin

                @pl.when(d != last_d)
                def _(up=up):
                    self.full(up, n).wait_send()

                @pl.when(d == last_d)
                def _(up=up, origin=origin):
                    self.half(up, n, origin).wait_send()

            for origin in range(2):
                self.core(origin, n).wait_send()
            return carry

        lax.fori_loop(0, self.count, one, 0)


class GramReduce:
    def __init__(self, place, sems, spread, keep, bufs, full):
        self.place, self.sems, self.spread = place, sems, spread
        self.keep, self.bufs, self.full = keep, bufs, full
        self.s = sems.take(10 * full.shape[0])
        self.right, self.left = place.at(dx=1), place.at(dx=-1)
        self.rows = full.shape[2]
        self.half = self.rows // 2
        self.lo, self.hi = pl.ds(0, self.half), pl.ds(self.half, self.half)

    def sc(self, r, i):
        diag, got, to_r, to_l, from_l, from_r = [self.bufs.at[r, k] for k in range(6)]
        src, dst, part, device = (
            (diag, got, self.lo, self.right),
            (diag, got, self.hi, self.left),
            (to_r, from_l, self.hi, self.right),
            (to_r, from_l, self.lo, self.right),
            (to_l, from_r, self.lo, self.left),
            (to_l, from_r, self.hi, self.left),
        )[i]
        return self.sems.copy(src.at[part], dst.at[part], self.s + 10 * r + i, device)

    def ga(self, r, i):
        x = self.place.x
        slot, part, device = (
            (x, pl.ds(0, self.rows), self.right),
            (x, pl.ds(0, self.rows), self.left),
            ((x + 3) % 4, self.lo, self.right),
            ((x + 1) % 4, self.hi, self.left),
        )[i]
        ref = self.full.at[r, slot, part]
        return self.sems.copy(ref, ref, self.s + 10 * r + 6 + i, device)

    def mine(self, r, i, part):
        first = i * self.rows + part * self.half
        return self.keep[r, pl.ds(pl.multiple_of(first, self.half), self.half)]

    def stage(self, number, r):
        x = self.place.x
        if number == 0:
            self.spread.arrived(r)
            bt, at = self.spread.bt, self.spread.at
            wide = at.shape[2] * at.shape[3] * at.shape[4]
            total = None
            for q in range(at.shape[1]):
                term = dot_nt(bt[q], at[r, q].reshape(wide, at.shape[5]))
                total = term if total is None else total + term
            self.keep[r] = total
            for part, rows in ((0, self.lo), (1, self.hi)):
                self.bufs[r, 0, rows] = self.mine(r, (x + 2) % 4, part).astype(BF)
            self.sc(r, 0).start()
            self.sc(r, 1).start()
            self.bufs[r, 2, self.hi] = self.mine(r, (x + 1) % 4, 1).astype(BF)
            self.sc(r, 2).start()
            self.bufs[r, 3, self.lo] = self.mine(r, (x + 3) % 4, 0).astype(BF)
            self.sc(r, 4).start()
        elif number == 1:
            self.sc(r, 0).wait_recv()
            got = self.bufs[r, 1, self.lo].astype(F32)
            self.bufs[r, 2, self.lo] = (self.mine(r, (x + 1) % 4, 0) + got).astype(BF)
            self.sc(r, 3).start()
            self.sc(r, 1).wait_recv()
            got = self.bufs[r, 1, self.hi].astype(F32)
            self.bufs[r, 3, self.hi] = (self.mine(r, (x + 3) % 4, 1) + got).astype(BF)
            self.sc(r, 5).start()
        elif number == 2:
            for i in (2, 3, 4, 5):
                self.sc(r, i).wait_recv()
            for part, rows in ((0, self.lo), (1, self.hi)):
                total = self.mine(r, x, part) + self.bufs[r, 4, rows].astype(F32) + self.bufs[r, 5, rows].astype(F32)
                self.full[r, x, rows] = total.astype(BF)
            self.ga(r, 0).start()
            self.ga(r, 1).start()
        elif number == 3:
            self.ga(r, 0).wait_recv()
            self.ga(r, 2).start()
            self.ga(r, 1).wait_recv()
            self.ga(r, 3).start()
        else:
            self.ga(r, 2).wait_recv()
            self.ga(r, 3).wait_recv()
            for i in range(6):
                self.sc(r, i).wait_send()
            for i in range(4):
                self.ga(r, i).wait_send()


def share_sum(place, sems, mine, slots, partners):
    s = sems.take(len(partners))
    copies = [sems.copy(mine, slots.at[i], s + i, device) for i, device in enumerate(partners)]
    for c in copies:
        c.start()
    return copies


def finish_sum(copies, mine, slots):
    for c in copies:
        c.wait()
    total = mine[...]
    for i in range(len(copies)):
        total = total + slots[i]
    return total


def main_kernel(
    prior_scale, width, rebuilt, e_far, rot_far, out,
    e, rot, near, wt, err, err_in, part_a, part_b, big, small, own_a, own_b, ab, ab_out, ab_in, xo, red,
    bt, at, gkeep, gbuf, gfull, yk, ybuf, sq, sq_in, last_out, last_in,
    send, recv,
):
    tok_rows = e.shape[0]
    step_rows = tok_rows // 2
    staged = [pltpu.make_async_copy(rot_far, rot, near.at[0])]
    for i in range(2):
        rows = pl.ds(i * step_rows, step_rows)
        staged.append(pltpu.make_async_copy(e_far.at[rows], e.at[rows], near.at[1 + i]))
    for copy in staged:
        copy.start()
    place = Place()
    sems = Sems(send, recv)
    barrier = pltpu.get_barrier_semaphore()
    col_peers = [place.col_peer(i) for i in range(1, NZL * NC)]
    partners = (
        [place.at(dx=i) for i in (1, 2, 3)]
        + [place.at(dy=i) for i in (1, 2, 3)]
        + [place.other_end(i) for i in range(NZL)]
        + col_peers
    )
    for device in partners:
        pl.semaphore_signal(barrier, inc=1, device_id=device, device_id_type=MESH)

    staged[0].wait()
    for first in range(0, tok_rows, step_rows):
        staged[1 + first // step_rows].wait()
        rotated = dot_nn(e[first : first + step_rows], rot[...])
        residue = rotated.T - rebuilt[:, first : first + step_rows]
        squares = residue * residue
        err[:, first : first + step_rows] = jnp.sum(squares, axis=0, keepdims=True)
    pl.semaphore_wait(barrier, len(partners))

    total = finish_sum(share_sum(place, sems, err, err_in, col_peers), err, err_in)
    weights = 1.0 / (1.0 + total / (2.0 * width))
    wt[...] = (rebuilt[...] * weights).astype(BF)

    block = out.shape[2]
    n_half = wt.shape[0] // 2
    x_cols = e.shape[1] // NX

    def compute_a(xi):
        start = pl.multiple_of(xi * x_cols, x_cols)
        value = dot_nn(wt[0:n_half], e[:, pl.ds(start, x_cols)])
        for zh in range(NZH):
            for y in range(NY):
                at_in, at_out = (zh * NY + y) * block, (y * NZH + zh) * block
                part_a[xi, :, at_out : at_out + block] = value[:, at_in : at_in + block]

    def compute_b(yi):
        parts = []
        for x in range(NX):
            for zh in range(NZH):
                start = pl.multiple_of(x * x_cols + (zh * NY + yi) * block, block)
                parts.append(e[:, pl.ds(start, block)])
        part_b[yi] = dot_nn(wt[n_half:], jnp.concatenate(parts, axis=1))

    sub = n_half // SUB
    m = ab.shape[2]

    def chain(which, k):
        first_axis, second_axis = ("x", "y") if which == 0 else ("y", "x")
        source, own = (part_a, own_a) if which == 0 else (part_b, own_b)
        prepare = (compute_a if which == 0 else compute_b) if k == 0 else None

        def keep_own(rows, total):
            own[rows] = total

        def keep_ab(rows, total):
            ab[which, rows] = total

        yield from ring_scatter(
            place, sems, first_axis, lambda i, rows: source[i, rows], keep_own,
            [big.at[which, i] for i in range(6)], k * sub, sub, prepare,
        )
        yield from ring_scatter(
            place, sems, second_axis, lambda i, rows: own[rows, pl.ds(pl.multiple_of(i * m, m), m)], keep_ab,
            [small.at[which, i] for i in range(6)], k * sub, sub,
        )

    def in_rounds(groups, finished, between=None):
        groups = dict(enumerate(groups))
        count = 0
        while groups:
            if between is not None:
                between(count)
            count += 1
            for k in list(groups):
                pump(groups[k])
                if not groups[k]:
                    del groups[k]
                    finished(k)

    swaps = []

    def start_swap(k):
        rows = pl.ds(k * sub, sub)
        ab_out[rows] = ab[1 - place.zh, rows].astype(BF)
        swap = sems.copy(ab_out.at[rows], ab_in.at[rows], sems.take(), place.at(dz=4))
        swap.start()
        swaps.append(swap)

    def add_prior(count):
        if count == 2:
            for zh in range(NZH):
                rows = pl.ds(pl.multiple_of(place.x * x_cols + (zh * NY + place.y) * block, block), block)
                cols = pl.ds(pl.multiple_of(place.zh * n_half, n_half), n_half)
                xo[:, zh * block : (zh + 1) * block] = prior_scale * rot[rows, cols].astype(F32).T

    in_rounds([[chain(0, k), chain(1, k)] for k in range(SUB)], start_swap, add_prior)

    parts, rows_r = at.shape[1], at.shape[5]
    wide = NZH * NC * rows_r
    panels = {0: [], 1: []}

    def share_rows(step, k):
        rows = pl.ds(k * sub, sub)
        bt[step, place.y, rows] = xo[rows].astype(BF)
        for r in range(k * parts // SUB, (k + 1) * parts // SUB):
            g = ring_gather(place, sems, "y", bt.at[step], r * rows_r, rows_r)
            next(g)
            panels[step].append(g)

    for k in range(SUB):
        rows = pl.ds(k * sub, sub)
        swaps[k].wait()
        xo[rows] = ab[place.zh, rows] + ab_in[rows].astype(F32) + xo[rows]
        share_rows(0, k)
    squares = xo[...] * xo[...]
    folded = jnp.sum(squares.reshape(squares.shape[0] // 8, 8, squares.shape[1]), axis=0)
    part = folded[:, 0:128]
    for i in range(1, folded.shape[1] // 128):
        part = part + folded[:, i * 128 : (i + 1) * 128]
    sq[0] = part

    y_copies = share_sum(place, sems, sq.at[0], sq_in.at[0], [place.at(dy=i) for i in (1, 2, 3)])
    mine = pl.ds(pl.multiple_of(place.zh * block, block), block)
    theirs = pl.ds(pl.multiple_of((1 - place.zh) * block, block), block)
    last = []
    spreads = []
    for step in range(2):
        b_ref, a_ref, g_ref = bt.at[step], at.at[step], gfull.at[step]
        panel = panels[step]
        spread = Spread(place, sems, b_ref, a_ref)
        spreads.append(spread)
        grams = GramReduce(place, sems, spread, gkeep, gbuf.at[step], g_ref)
        per, gap, stages = spread.slots, spread.slots * GAP, 5
        d = spread.d
        hops = 4 - d + (d // 3) * 2

        def after(t):
            for number in reversed(range(stages)):
                ahead = t - gap * number - (per - 1) - LAG * hops

                @pl.when((ahead >= 0) & (ahead % per == 0) & (ahead < per * parts))
                def _(number=number, ahead=ahead):
                    grams.stage(number, ahead // per)

        run(panel[0])
        for g in panel[1:]:
            next(g)
        for r in range(1, parts):
            spread.steps((r - 1) * per, r * per)
            run(panel[r])
        if step == 0:
            sq[1] = finish_sum(y_copies, sq.at[0], sq_in.at[0])
            z_copies = share_sum(place, sems, sq.at[1], sq_in.at[1], [place.at(dz=i) for i in range(1, 8)])
        spread.steps((parts - 1) * per, parts * per + LAG * 4 + gap * (stages - 1), after)
        if step == 0:
            sq[2] = finish_sum(z_copies, sq.at[1], sq_in.at[1])
            c_copies = share_sum(place, sems, sq.at[2], sq_in.at[2], [place.at(dc=1)])

        def compute_y(q):
            value = None
            for r in range(parts):
                gram = jnp.concatenate([g_ref[r, i] for i in range(NX)], axis=0)
                term = dot_nn(gram, a_ref[r, q].reshape(wide, a_ref.shape[5]))
                value = term if value is None else value + term
            yk[q] = value

        def keep_y(rows, total):
            red[rows] = total

        def sums(count, step=step):
            if step == 0 and count == 1:
                sq[3] = finish_sum(shared["c"], sq.at[2], sq_in.at[2])
                shared["x"] = share_sum(place, sems, sq.at[3], sq_in.at[3], [place.at(dx=i) for i in (1, 2, 3)])
            if step == 0 and count == 3:
                total = jnp.sum(finish_sum(shared["x"], sq.at[3], sq_in.at[3]))
                scale2 = jnp.full((8, 128), 1.96 / width, F32) * total
                shared["inv"] = jnp.tile((1.0 / jnp.sqrt(scale2))[0:1], (1, m // 128))

        def finish_rows(k, step=step):
            rows = pl.ds(k * sub, sub)
            if step == 0:
                f = shared["inv"]
                xo[rows] = (1.5 * xo[rows] - 0.5 * (red[rows] * (f * f))) * f
                share_rows(1, k)
            else:
                xo[rows] = math.sqrt(width) * (1.5 * xo[rows] - 0.5 * red[rows])
                last_out[rows] = xo[rows, theirs].astype(BF)
                swap = sems.copy(last_out.at[rows], last_in.at[rows], sems.take(), place.at(dz=4))
                swap.start()
                last.append(swap)
                out[place.zh, rows] = xo[rows, mine]

        shared = {"c": c_copies if step == 0 else None}
        in_rounds(
            [
                [
                    ring_scatter(
                        place, sems, "y", lambda i, rows: yk[i, rows], keep_y,
                        [ybuf.at[step, i] for i in range(6)], k * sub, sub, compute_y if k == 0 else None,
                    )
                ]
                for k in range(SUB)
            ],
            finish_rows,
            sums,
        )
    for spread in spreads:
        spread.sent()
    for k in range(SUB):
        rows = pl.ds(k * sub, sub)
        last[k].wait()
        out[1 - place.zh, rows] = last_in[rows].astype(F32)


def shards(embeddings, rotation, codes, codebooks):
    tok_rows, width = embeddings.shape
    cols = rotation.shape[1]
    subs, centroids, sub_width = codebooks.shape
    rows_total = tok_rows * lax.axis_size("dp")
    block = width // lax.axis_size("dp")
    rebuilt = pl.pallas_call(
        rebuild_kernel,
        out_shape=jax.ShapeDtypeStruct((subs, sub_width, tok_rows), F32),
        in_specs=[pl.BlockSpec(memory_space=pltpu.VMEM)] * 2,
        out_specs=pl.BlockSpec(memory_space=pltpu.VMEM),
        name="rebuild",
    )(codes.T, codebooks.transpose(0, 2, 1)).reshape(cols, tok_rows)
    n = cols // NZH
    m = NZH * block
    panel = m * NY
    parts = PARTS
    rows = n // parts
    wide = NZH * NC * rows
    vm = pltpu.VMEM
    out_t = pl.pallas_call(
        functools.partial(main_kernel, 0.2 * rows_total, width),
        out_shape=jax.ShapeDtypeStruct((NZH, n, block), F32),
        in_specs=[pl.BlockSpec(memory_space=pltpu.VMEM)] + [pl.BlockSpec(memory_space=pl.ANY)] * 2,
        out_specs=pl.BlockSpec(memory_space=pltpu.VMEM),
        scratch_shapes=[
            vm((tok_rows, width), BF), vm((width, cols), BF), pltpu.SemaphoreType.DMA((3,)),
            vm((cols, tok_rows), BF), vm((1, tok_rows), F32), vm((NZL * NC - 1, 1, tok_rows), F32),
            vm((NX, n, panel), F32), vm((NY, n, panel), F32),
            vm((2, 6, n, panel), BF), vm((2, 6, n, m), BF),
            vm((n, panel), F32), vm((n, panel), F32),
            vm((2, n, m), F32), vm((n, m), BF), vm((n, m), BF),
            vm((n, m), F32), vm((n, m), F32),
            vm((2, NY, n, m), BF), vm((2, parts, NY, NZH, NC, rows, m), BF),
            vm((parts, n, wide), F32), vm((2, parts, 6, n // NX, wide), BF),
            vm((2, parts, NX, n // NX, wide), BF),
            vm((NY, n, m), F32), vm((2, 6, n, m), BF),
            vm((4, 8, 128), F32), vm((4, 7, 8, 128), F32),
            vm((n, block), BF), vm((n, block), BF),
            pltpu.SemaphoreType.DMA((NSEM,)), pltpu.SemaphoreType.DMA((NSEM,)),
        ],
        compiler_params=pltpu.CompilerParams(collective_id=0, has_side_effects=True, vmem_limit_bytes=60 * 2**20),
        name="main",
    )(rebuilt, embeddings, rotation)
    return out_t.reshape(cols, block).T


def solution(mesh):
    placed = (P("dp", None), P(None, "col"), P("dp", "col"), P("col", None, None))
    return jax.shard_map(
        shards, mesh=mesh, in_specs=placed, out_specs=P("dp", "col"), check_vma=False
    )
```
